256 devices in a mesh: ctx: 32 (over y_hi, z, core), exp: 8 (over y_lo, x).
Axes of the slice: x: 4, y: 4 (y_hi: 2, y_lo: 2; y = y_hi * 2 + y_lo), z: 8, core: 2. Of those that a mesh axis runs over, the one named last changes fastest.
Arguments:
- queries: bfloat16 [4096, 4096], P('ctx', 'exp'), may hold values from -96 to 96
- keys: bfloat16 [4096, 512], P('ctx'), may hold values from -4 to 4
- values: bfloat16 [4096, 512], P('ctx'), may hold values from -5 to 5
- span_order: int32 [64], replicated, may hold values from 0 to 63, each once
- stream_in: bfloat16 [4096, 2048], P(('ctx', 'exp')), may hold values from -12 to 12
- wo: bfloat16 [32, 128, 2048], P('exp', None, 'ctx'), may hold values from -0.09375 to 0.09375
- norm_gain: bfloat16 [2048], replicated, may hold values from 0.5 to 1.5
- expert_ids: int32 [4096, 8], P(('ctx', 'exp')), may hold values from 0 to 127, all different within a row; in each aligned block of 16 rows (0 to 15, 16 to 31, ...) at most 2 rows name the same one
- expert_gates: bfloat16 [4096, 8], P(('ctx', 'exp')), may hold values from 0.019897461 to 0.5
- w_gate: bfloat16 [128, 2048, 768], P('exp', 'ctx'), may hold values from -0.125 to 0.125
- w_up: bfloat16 [128, 2048, 768], P('exp', 'ctx'), may hold values from -0.125 to 0.125
- w_down: bfloat16 [128, 2048, 768], P('exp', 'ctx'), may hold values from -0.21875 to 0.21875
Outputs:
- layer_out: float32 [4096, 2048], P(('ctx', 'exp'))
The draws below stay inside these ranges and needn't reach their ends.
Inputs may be any that keep to these rules, and one draw needn't show every extreme that they name: `span_order`: each value 0 to 63 appears once. `expert_ids`: each row names 8 different experts. Among the 16 rows of one device (aligned blocks), no expert is named more than 2 times, a bound that some block reaches.
All inputs are finite; a program needn't handle non-finite values.
Results may differ from the reference program's by a relative error of at most 0.005.
Values may be sent and summed in bfloat16 or wider, within the bound.
No kernel may reach another device: no remote copies, remote signals or barrier semaphores. Data moves between devices by JAX's collectives and lax.ppermute only.
A program may use at most 64 MiB of HBM per device.

```python
import math
import jax
import jax.numpy as jnp
import numpy as np
from jax import lax

D = 2048
FF = 768
QH = 32
KVH = 4
HD = 128
TOPK = 8
EXPERTS = 128
SPAN = 64
LENGTH = 4096
ROWS_DEV = 16
CAP = 2
GROUP = 8
N_CTX = 32


def draw_keys(key, part):
    out = jnp.clip(jax.random.normal(jax.random.fold_in(key, 11), (LENGTH, KVH * HD), jnp.float32), -4.0, 4.0)
    return out.astype(jnp.bfloat16)


def draw_queries(key, part):
    out = 2.0 * jnp.clip(jax.random.normal(jax.random.fold_in(key, 12), (LENGTH, QH * HD), jnp.float32), -4.0, 4.0)
    return out.astype(jnp.bfloat16)


def draw_stream_in(key, part):
    row_scale = 0.3 * jnp.exp(jax.random.uniform(jax.random.fold_in(key, 22), (LENGTH, 1), jnp.float32) * math.log(10.0))
    base = jnp.clip(jax.random.normal(jax.random.fold_in(key, 21), (LENGTH, D), jnp.float32), -4.0, 4.0)
    out = base * row_scale
    return out.astype(jnp.bfloat16)


def levels(stream_key, shape, split, least, largest):
    def one(axis_at, blocks):
        draws = jax.random.uniform(jax.random.fold_in(jax.random.fold_in(stream_key, 6), axis_at), (blocks,), jnp.float32, least / len(split), largest / len(split))
        return jnp.repeat(jnp.exp(draws), shape[axis_at] // blocks).reshape((-1,) + (1,) * (len(shape) - axis_at - 1))

    level = one(*split[0])
    for cut in split[1:]:
        level = level * one(*cut)
    return level


def assign_block(own_key, own, number, rows, count, top, bound, slope):
    sequence = jax.random.permutation(own_key, count)
    packed, common = portions_of(count, rows * top, bound, slope, True), portions_of(count, rows * top, bound, slope, False)
    places = jnp.arange(count)

    def named(sizes, offset_by):
        used = int((sizes > 0).sum())
        fixed = max(1, used // 4)
        passed = fixed + (places - fixed + offset_by * (used - fixed)) % max(1, count - fixed)
        return jnp.zeros((count,), jnp.int32).at[sequence[jnp.where(places < fixed, places, passed)]].set(jnp.asarray(sizes, jnp.int32))

    sizes = jnp.where(number % 4 == 0, named(packed, number // 4), named(common, number - number // 4 - 1))
    mixed = jax.random.permutation(jax.random.fold_in(own, 3), count)
    donor, taker = mixed[0:count // 2 * 2:2], mixed[1:count // 2 * 2:2]
    margin = jnp.minimum(sizes[donor] - 1, bound - sizes[taker]) // 2
    margin = jnp.where((donor == sequence[0]) | (taker == sequence[0]) | (sizes[taker] == 0), 0, jnp.maximum(margin, 0))
    passed = jax.random.randint(jax.random.fold_in(own, 4), (count // 2,), 0, 1 << 20) % (margin + 1)
    sizes = sizes.at[donor].add(-passed).at[taker].add(passed)
    members = jnp.searchsorted(jnp.cumsum(sizes), jnp.arange(rows * top), side="right").astype(jnp.int32)
    grid = members.reshape(top, rows).T
    grid = grid[jax.random.permutation(jax.random.fold_in(own, 1), rows)]
    offset_by = jax.random.randint(jax.random.fold_in(own, 2), (rows, 1), 0, top)
    return jnp.take_along_axis(grid, (jnp.arange(top)[None, :] + offset_by) % top, axis=1)


def portions_of(count, total, most, skew, full):
    loads = [(1 << 20) // math.isqrt(grade ** skew) + 1 for grade in range(1, count + 1)]
    largest = most if full else min(most, max(-(-total // count), total * loads[0] // sum(loads)))
    least = 1 if total - largest >= count - 1 else 0
    holding, surplus = [largest] + [least] * (count - 1), total - largest - least * (count - 1)
    while surplus > 0:
        movable = [i for i in range(1, count) if holding[i] < largest] or [i for i in range(1, count) if holding[i] < most]
        mass, budget = sum([loads[i] for i in movable]), surplus
        for i in movable:
            more = min(most - holding[i], max(1, budget * loads[i] // mass), surplus)
            holding[i] = holding[i] + more
            surplus = surplus - more
    return np.array(holding)


def bell_draw(rng, dims, deviation, most, cuts=(), held_as=jnp.bfloat16):
    drawn = jax.random.normal(rng, dims, jnp.float32) * deviation
    if len(cuts) > 0:
        drawn = levels(rng, dims, cuts, -0.22, 0.18) * drawn
    return jnp.clip(drawn, min=-most, max=most).astype(held_as)


def setup_inputs(seed: int = 0) -> dict:
    key_list = jax.random.split(jax.random.key(seed), 13)
    queries = draw_queries(jax.random.fold_in(key_list[12], 71), 0)
    keys = draw_keys(jax.random.fold_in(key_list[12], 71), 0)
    values = bell_draw(key_list[2], (LENGTH, KVH * HD), 1.0, 5.0, ((0, 32),))
    span_order = jax.random.permutation(key_list[3], 2 * N_CTX).astype(jnp.int32)
    stream_in = draw_stream_in(jax.random.fold_in(key_list[12], 71), 0)
    wo = bell_draw(key_list[5], (QH, HD, D), (QH * HD) ** -0.5, 0.09375, ((0, 8), (2, 32)))
    norm_gain = jnp.clip(1.0 + 0.1 * jax.random.normal(key_list[6], (D,), jnp.float32), 0.5, 1.5).astype(jnp.bfloat16)
    expert_ids_keys = jax.random.split(jax.random.fold_in(key_list[7], 1), LENGTH // ROWS_DEV)
    expert_ids_turns = jax.random.permutation(jax.random.fold_in(key_list[7], 3), LENGTH // ROWS_DEV)
    expert_ids = jax.vmap(lambda own, number: assign_block(jax.random.fold_in(key_list[7], 2), own, number, ROWS_DEV, EXPERTS, TOPK, CAP, 2))(expert_ids_keys, expert_ids_turns).reshape((LENGTH, TOPK))
    expert_gates = jnp.clip(jnp.exp(math.log(0.5) - 3.224016 * jax.random.uniform(key_list[8], (LENGTH, TOPK), jnp.float32) ** levels(key_list[8], (LENGTH, TOPK), ((0, 256),), -0.2, 0.2)), 0.019897461, 0.5).astype(jnp.bfloat16)
    w_gate = bell_draw(key_list[9], (EXPERTS, D, FF), D ** -0.5, 0.125, ((0, 8), (1, 32)))
    w_up = bell_draw(key_list[10], (EXPERTS, D, FF), D ** -0.5, 0.125, ((0, 8), (1, 32)))
    w_down = bell_draw(key_list[11], (EXPERTS, D, FF), FF ** -0.5, 0.21875, ((0, 8), (1, 32)))
    return {"queries": queries, "keys": keys, "values": values, "span_order": span_order, "stream_in": stream_in, "wo": wo, "norm_gain": norm_gain, "expert_ids": expert_ids, "expert_gates": expert_gates, "w_gate": w_gate, "w_up": w_up, "w_down": w_down}


def expert_apply(tokens, gate_w, up_w, down_w):
    gate_part = jnp.dot(tokens, gate_w, preferred_element_type=jnp.float32)
    up_part = jnp.dot(tokens, up_w, preferred_element_type=jnp.float32)
    active = (jax.nn.silu(gate_part) * up_part).astype(jnp.bfloat16)
    return lax.dot_general(active, down_w, (((1,), (1,)), ((), ())), preferred_element_type=jnp.float32)

def reference(queries, keys, values, span_order, stream_in, wo, norm_gain, expert_ids, expert_gates, w_gate, w_up, w_down):
    row_ids = jnp.arange(LENGTH, dtype=jnp.int32)
    place = span_order[row_ids // SPAN] * SPAN + row_ids % SPAN
    block = min(512, LENGTH)
    scale = 1.0 / math.sqrt(HD)
    query_blocks = queries.reshape(LENGTH // block, block, QH * HD)
    place_blocks = place.reshape(LENGTH // block, block)

    def attend_block(item):
        query_rows, query_place = item
        visible = place[None, None, :] <= query_place[None, :, None]
        heads = []
        for kv_head in range(KVH):
            query_part = query_rows[:, kv_head * GROUP * HD:(kv_head + 1) * GROUP * HD].reshape(block, GROUP, HD).astype(jnp.float32)
            key_part = keys[:, kv_head * HD:(kv_head + 1) * HD].astype(jnp.float32)
            value_part = values[:, kv_head * HD:(kv_head + 1) * HD].astype(jnp.float32)
            scores = jnp.einsum('qgd,nd->gqn', query_part, key_part) * scale
            scores = jnp.where(visible, scores, -jnp.inf)
            top = lax.optimization_barrier(jnp.max(scores, axis=-1, keepdims=True))
            probs = jnp.exp(scores - top)
            total = lax.optimization_barrier(jnp.sum(probs, axis=-1))
            probs_low = lax.optimization_barrier(probs.astype(jnp.bfloat16))
            summed = jnp.einsum('gqn,nd->qgd', probs_low.astype(jnp.float32), value_part)
            heads.append((summed / jnp.transpose(total)[:, :, None]).reshape(block, GROUP * HD))
        return jnp.concatenate(heads, axis=1).astype(jnp.bfloat16)
    attended = lax.map(attend_block, (query_blocks, place_blocks)).reshape(LENGTH, QH * HD)
    mixed = jnp.dot(attended, wo.reshape(QH * HD, D), preferred_element_type=jnp.float32)
    resid = stream_in.astype(jnp.float32) + mixed
    normed = (resid * lax.rsqrt(lax.optimization_barrier(jnp.mean(resid * resid, axis=-1, keepdims=True)) + 1e-06) * norm_gain.astype(jnp.float32)).astype(jnp.bfloat16)
    blocks = LENGTH // ROWS_DEV
    chosen = expert_ids.reshape(blocks, ROWS_DEV * TOPK)
    hits = (chosen[..., None] == jnp.arange(EXPERTS, dtype=jnp.int32)).astype(jnp.int32)
    rank = lax.optimization_barrier(jnp.sum((jnp.cumsum(hits, axis=1) - hits) * hits, axis=-1)).astype(jnp.int32)
    block_ids = jnp.arange(blocks, dtype=jnp.int32)[:, None]
    target = chosen * (blocks * CAP) + block_ids * CAP + rank
    source_row = block_ids * ROWS_DEV + jnp.arange(ROWS_DEV * TOPK, dtype=jnp.int32)[None, :] // TOPK
    table = jnp.full((EXPERTS * blocks * CAP,), LENGTH, jnp.int32).at[target.reshape(-1)].set(source_row.reshape(-1).astype(jnp.int32)).reshape(EXPERTS, blocks * CAP)
    gate_table = jnp.zeros((EXPERTS * blocks * CAP,), jnp.float32).at[target.reshape(-1)].set(expert_gates.reshape(-1).astype(jnp.float32)).reshape(EXPERTS, blocks * CAP)
    padded = jnp.concatenate([normed, jnp.zeros((1, D), jnp.bfloat16)], axis=0)

    def expert_step(total, item):
        slot_rows, slot_gates, gate_w, up_w, down_w = item
        tokens = padded[slot_rows]
        result = lax.optimization_barrier(expert_apply(tokens, gate_w, up_w, down_w).astype(jnp.bfloat16))
        contrib = slot_gates[:, None] * result.astype(jnp.float32)
        return (total.at[slot_rows].add(contrib), None)
    start_total = jnp.zeros((LENGTH + 1, D), jnp.float32)
    moe, _ = lax.scan(expert_step, start_total, (table, gate_table, w_gate, w_up, w_down))
    return resid + moe[:LENGTH]
```

```python
import math

import jax
import jax.numpy as jnp
from jax import lax
from jax.experimental import pallas as pl
from jax.experimental.pallas import tpu as pltpu
from jax.sharding import Mesh
from jax.sharding import PartitionSpec as P

D = 2048
HALF = D // 2
HD = 128
TOPK = 8
SPAN = 64
EXPERTS = 128
OWN = 16
CAP = 2
CHIP = ("yh", "z")
CTX = ("yh", "z", "core")
ALL = ("yh", "z", "core", "exp")
NEG_BIG = -1e30
SWAP = [(0, 1), (1, 0)]


def swapped(x):
    return lax.ppermute(x, "core", SWAP)


def attend_kernel(span_ref, ctx_ref, q_ref, near_ref, far_ref, o_ref, s_ref):
    ctx = ctx_ref[0]
    core = lax.rem(ctx, 2)
    rows = q_ref.shape[0]
    part = near_ref.shape[0]
    q = q_ref[...]
    row = lax.broadcasted_iota(jnp.int32, (rows, 1), 0)
    q_place = jnp.where(
        row < SPAN,
        span_ref[2 * ctx] * SPAN + row,
        span_ref[2 * ctx + 1] * SPAN + row - SPAN,
    )
    lane = lax.broadcasted_iota(jnp.int32, (1, 2 * SPAN), 1)
    dims = (((1,), (1,)), ((), ()))
    top = jnp.full((rows, 128), NEG_BIG, jnp.float32)
    blocks = part // 128
    for side, ref in enumerate((near_ref, far_ref)):
        held = jnp.where(side == 0, core, 1 - core)
        for b in range(blocks):
            k = ref[b * 128 : (b + 1) * 128, 0:HD]
            s = lax.dot_general(q, k, dims, preferred_element_type=jnp.float32)
            at = 2 * (2 * b + held)
            place = jnp.where(
                lane < SPAN,
                span_ref[at] * SPAN + lane,
                span_ref[at + 1] * SPAN + lane - SPAN,
            )
            s = jnp.where(place <= q_place, s, NEG_BIG)
            c0 = (side * blocks + b) * 128
            s_ref[:, c0 : c0 + 128] = s
            top = jnp.maximum(top, s)
    top = jnp.max(top, axis=1, keepdims=True)
    scale = math.log2(math.e) / math.sqrt(HD)
    total = jnp.zeros((rows, 128), jnp.float32)
    acc = jnp.zeros((rows, HD), jnp.float32)
    wide = 512
    for side, ref in enumerate((near_ref, far_ref)):
        for b in range(part // wide):
            c0 = side * part + b * wide
            p = jnp.exp2((s_ref[:, c0 : c0 + wide] - top) * scale)
            for j in range(wide // 128):
                total = total + p[:, j * 128 : (j + 1) * 128]
            v = ref[b * wide : (b + 1) * wide, HD : 2 * HD]
            acc = acc + jnp.dot(p.astype(jnp.bfloat16), v, preferred_element_type=jnp.float32)
    o_ref[...] = (acc / jnp.sum(total, axis=1, keepdims=True)).astype(o_ref.dtype)


def attend(span_order, ctx, queries, near, far):
    rows, width = queries.shape
    keys = near.shape[0] + far.shape[0]
    return pl.pallas_call(
        attend_kernel,
        out_shape=jax.ShapeDtypeStruct((rows, width), jnp.bfloat16),
        grid_spec=pltpu.PrefetchScalarGridSpec(
            num_scalar_prefetch=2,
            grid=(width // HD,),
            in_specs=[
                pl.BlockSpec((rows, HD), lambda h, *_: (0, h)),
                pl.BlockSpec(near.shape, lambda h, *_: (0, 0)),
                pl.BlockSpec(far.shape, lambda h, *_: (0, 0)),
            ],
            out_specs=pl.BlockSpec((rows, HD), lambda h, *_: (0, h)),
            scratch_shapes=[pltpu.VMEM((rows, keys), jnp.float32)],
        ),
        cost_estimate=pl.CostEstimate(
            flops=4 * rows * width * keys,
            bytes_accessed=4 * keys * HD * 2 + 4 * rows * width,
            transcendentals=rows * keys * width // HD,
        ),
    )(span_order, ctx, queries, near, far)


def copies(x, axes):
    count = lax.axis_size(axes)
    return jnp.broadcast_to(x[None], (count, *x.shape))


def gathered(x):
    near = lax.all_to_all(copies(x, CHIP), CHIP, 0, 0, tiled=True)
    near = near.reshape(-1, x.shape[-1])
    return near, swapped(near)


def by_plane(x):
    rows = x.shape[0]
    return x.reshape(rows, D // 128, 2, 64).transpose(0, 2, 1, 3).reshape(rows, D)


def from_planes(x):
    rows = x.shape[0]
    return x.reshape(rows, 2, D // 128, 64).transpose(0, 2, 1, 3).reshape(rows, D)


def shards(
    queries,
    keys,
    values,
    span_order,
    stream_in,
    wo,
    norm_gain,
    expert_ids,
    expert_gates,
    w_gate,
    w_up,
    w_down,
):
    core = lax.axis_index("core")
    ctx = lax.axis_index(CTX)
    exp = lax.axis_index("exp")

    gate_w = lax.all_to_all(w_gate, CHIP, 0, 0, tiled=True)
    up_w = lax.all_to_all(w_up, CHIP, 0, 0, tiled=True)
    down_w = lax.all_to_all(w_down, CHIP, 0, 0, tiled=True)

    head = exp // 2 * HD
    mine = jnp.concatenate(
        [
            lax.dynamic_slice_in_dim(keys, head, HD, 1),
            lax.dynamic_slice_in_dim(values, head, HD, 1),
        ],
        axis=1,
    )
    near, far = gathered(mine)
    wo_near, wo_far = gathered(wo.transpose(2, 0, 1).reshape(wo.shape[2], -1))

    attended = attend(span_order, ctx[None].astype(jnp.int32), queries, near, far)
    dims = (((1,), (1,)), ((), ()))
    a = lax.dot_general(attended, wo_near, dims, preferred_element_type=jnp.float32)
    b = lax.dot_general(attended, wo_far, dims, preferred_element_type=jnp.float32)
    mixed = jnp.concatenate(
        [jnp.where(core == 0, a, b), jnp.where(core == 0, b, a)], axis=1
    ).astype(jnp.bfloat16)
    mixed = lax.all_to_all(
        mixed.reshape(8, -1, D), "exp", 0, 0, tiled=True
    )
    resid = by_plane(stream_in.astype(jnp.float32)) + mixed.astype(jnp.float32).sum(axis=0)
    gain = by_plane(norm_gain.astype(jnp.float32)[None])
    normed = (
        resid
        * lax.rsqrt(jnp.mean(resid * resid, axis=-1, keepdims=True) + 1e-06)
        * gain
    ).astype(jnp.bfloat16)

    rows = stream_in.shape[0]
    flat = expert_ids.reshape(-1)
    hits = (flat[:, None] == jnp.arange(EXPERTS, dtype=jnp.int32)[None, :]).astype(jnp.float32)
    before = (
        jnp.arange(rows * TOPK)[:, None] > jnp.arange(rows * TOPK)[None, :]
    ).astype(jnp.float32)
    ahead = jnp.dot(before, hits, preferred_element_type=jnp.float32)
    rank = jnp.sum(ahead * hits, axis=1).astype(jnp.int32)
    slots = (((flat % OWN) * 8 + flat // OWN) * CAP + rank).reshape(rows, TOPK)
    slot_ids = jnp.arange(EXPERTS * CAP, dtype=jnp.int32)
    placing = jnp.any(slots[None, :, :] == slot_ids[:, None, None], axis=2).astype(jnp.bfloat16)
    combine = jnp.sum(
        jnp.where(
            slots[:, :, None] == slot_ids[None, None, :],
            expert_gates[:, :, None],
            jnp.zeros((), jnp.bfloat16),
        ),
        axis=1,
    )

    outgoing = jnp.dot(placing, normed, preferred_element_type=jnp.float32).astype(jnp.bfloat16)
    outgoing = (
        outgoing.reshape(OWN, 8, CAP, 2, HALF)
        .transpose(0, 3, 1, 2, 4)
        .reshape(256, CAP, HALF)
    )
    tokens = lax.all_to_all(outgoing, ALL, 0, 0, tiled=True).reshape(512, HALF)

    gate_w = gate_w.reshape(HALF, -1)
    up_w = up_w.reshape(HALF, -1)
    down_w = down_w.reshape(HALF, -1)
    g = jnp.dot(tokens, gate_w, preferred_element_type=jnp.float32)
    u = jnp.dot(tokens, up_w, preferred_element_type=jnp.float32)
    gu = jnp.concatenate([g, u], axis=1).reshape(2, 256, -1)
    keep = jnp.where(core == 0, gu[0], gu[1])
    send = jnp.where(core == 0, gu[1], gu[0])
    both = keep + swapped(send)
    width = both.shape[1] // 2
    act = (jax.nn.silu(both[:, :width]) * both[:, width:]).astype(jnp.bfloat16)
    act_other = swapped(act)
    act = jnp.concatenate(
        [jnp.where(core == 0, act, act_other), jnp.where(core == 0, act_other, act)],
        axis=0,
    )
    out = lax.dot_general(
        act, down_w, (((1,), (1,)), ((), ())), preferred_element_type=jnp.float32
    ).astype(jnp.bfloat16)
    home = lax.all_to_all(out.reshape(256, CAP, HALF), ALL, 0, 0, tiled=True)
    home = home.reshape(OWN, 2, 8, CAP, HALF).transpose(0, 2, 3, 1, 4).reshape(EXPERTS * CAP, D)
    moe = jnp.dot(combine, home, preferred_element_type=jnp.float32)
    return from_planes(resid + moe)


def solution(mesh):
    finer = Mesh(mesh.devices.reshape(2, 8, 2, 8), ALL)
    return jax.shard_map(
        shards,
        mesh=finer,
        in_specs=(
            P(CTX, "exp"),
            P(CTX, None),
            P(CTX, None),
            P(),
            P(ALL, None),
            P("exp", None, CTX),
            P(),
            P(ALL, None),
            P(ALL, None),
            P("exp", CTX, None),
            P("exp", CTX, None),
            P("exp", CTX, None),
        ),
        out_specs=P(ALL, None),
        check_vma=False,
    )
```

```python
import math

import jax
import jax.numpy as jnp
from jax import lax
from jax.experimental import pallas as pl
from jax.experimental.pallas import tpu as pltpu
from jax.sharding import Mesh
from jax.sharding import PartitionSpec as P


D = 2048
HALF = D // 2
HD = 128
TOPK = 8
SPAN = 64
EXPERTS = 128
OWN = 16
CAP = 2
CHIP = ("yh", "z")
CTX = ("yh", "z", "core")
ALL = ("yh", "z", "core", "exp")
NEG_BIG = -1e30
SWAP = [(0, 1), (1, 0)]


def swapped(x):
    return lax.ppermute(x, "core", SWAP)


def attend_pieces(span_ref, ctx, q_ref, keys, values, o_ref, s_ref):
    rows = q_ref.shape[0]
    part = keys[0].shape[0]
    blocks = part // 128
    yh = ctx // 16
    core = lax.rem(ctx, 2)
    q = q_ref[...]
    row = lax.broadcasted_iota(jnp.int32, (rows, 1), 0)
    q_place = jnp.where(
        row < SPAN,
        span_ref[2 * ctx] * SPAN + row,
        span_ref[2 * ctx + 1] * SPAN + row - SPAN,
    )
    lane = lax.broadcasted_iota(jnp.int32, (1, 2 * SPAN), 1)
    dims = (((1,), (1,)), ((), ()))
    top = jnp.full((rows, 128), NEG_BIG, jnp.float32)
    for side in range(4):
        first = (yh if side % 2 == 0 else 1 - yh) * 16 + (core if side < 2 else 1 - core)
        for b in range(blocks):
            k = keys[side][b * 128 : (b + 1) * 128, :]
            s = lax.dot_general(q, k, dims, preferred_element_type=jnp.float32)
            at = 2 * (first + 2 * b)
            place = jnp.where(
                lane < SPAN,
                span_ref[at] * SPAN + lane,
                span_ref[at + 1] * SPAN + lane - SPAN,
            )
            s = jnp.where(place <= q_place, s, NEG_BIG)
            c0 = (side * blocks + b) * 128
            s_ref[:, c0 : c0 + 128] = s
            top = jnp.maximum(top, s)
    top = jnp.max(top, axis=1, keepdims=True)
    scale = math.log2(math.e) / math.sqrt(HD)
    total = jnp.zeros((rows, 128), jnp.float32)
    acc = jnp.zeros((rows, HD), jnp.float32)
    wide = 512
    for side in range(4):
        for b in range(part // wide):
            c0 = side * part + b * wide
            p = jnp.exp2((s_ref[:, c0 : c0 + wide] - top) * scale)
            for j in range(wide // 128):
                total = total + p[:, j * 128 : (j + 1) * 128]
            v = values[side][b * wide : (b + 1) * wide, :]
            acc = acc + jnp.dot(p.astype(jnp.bfloat16), v, preferred_element_type=jnp.float32)
    o_ref[...] = (acc / jnp.sum(total, axis=1, keepdims=True)).astype(o_ref.dtype)


def attend_kernel(span_ref, where_ref, q_ref, *refs):
    own, cross = refs[0:4], refs[4:8]
    o_ref, s_ref = refs[8:]
    ctx = where_ref[0]

    @pl.when(where_ref[1] == 0)
    def _():
        attend_pieces(span_ref, ctx, q_ref, own, cross, o_ref, s_ref)

    @pl.when(where_ref[1] != 0)
    def _():
        attend_pieces(span_ref, ctx, q_ref, cross, own, o_ref, s_ref)


def attend(span_order, where, queries, own, cross):
    rows, width = queries.shape
    keys = 4 * own[0].shape[0]
    return pl.pallas_call(
        attend_kernel,
        out_shape=jax.ShapeDtypeStruct((rows, width), jnp.bfloat16),
        grid_spec=pltpu.PrefetchScalarGridSpec(
            num_scalar_prefetch=2,
            grid=(width // HD,),
            in_specs=[pl.BlockSpec((rows, HD), lambda h, *_: (0, h))]
            + [pl.BlockSpec(own[0].shape, lambda h, *_: (0, 0))] * 8,
            out_specs=pl.BlockSpec((rows, HD), lambda h, *_: (0, h)),
            scratch_shapes=[pltpu.VMEM((rows, keys), jnp.float32)],
        ),
        cost_estimate=pl.CostEstimate(
            flops=4 * rows * width * keys,
            bytes_accessed=4 * keys * HD + 4 * rows * width,
            transcendentals=rows * keys * width // HD,
        ),
    )(span_order, where, queries, *own, *cross)


def copies(x, axes):
    return jnp.broadcast_to(x[None], (lax.axis_size(axes), *x.shape))


def across_y(x):
    return lax.ppermute(x, "yh", SWAP)


def across_x(x):
    return lax.ppermute(x, "exp", [(e, e ^ 1) for e in range(8)])


def across_xy(x):
    pairs = [(y * 8 + e, (1 - y) * 8 + (e ^ 1)) for y in range(2) for e in range(8)]
    return lax.ppermute(x, ("yh", "exp"), pairs)


def by_plane(x):
    rows = x.shape[0]
    return x.reshape(rows, D // 128, 2, 64).transpose(0, 2, 1, 3).reshape(rows, D)


def from_planes(x):
    rows = x.shape[0]
    return x.reshape(rows, 2, D // 128, 64).transpose(0, 2, 1, 3).reshape(rows, D)


def shards(
    queries,
    keys,
    values,
    span_order,
    stream_in,
    wo,
    norm_gain,
    expert_ids,
    expert_gates,
    w_gate,
    w_up,
    w_down,
):
    core = lax.axis_index("core")
    ctx = lax.axis_index(CTX)
    exp = lax.axis_index("exp")
    yh = lax.axis_index("yh")

    head = exp // 2 * HD
    mine = jnp.where(
        exp % 2 == 0,
        lax.dynamic_slice_in_dim(keys, head, HD, 1),
        lax.dynamic_slice_in_dim(values, head, HD, 1),
    )
    packed = jnp.concatenate([mine, wo.transpose(0, 2, 1).reshape(-1, HD)], axis=0)
    packed = lax.all_to_all(copies(packed, "z"), "z", 0, 0, tiled=True)
    gate_up_w = lax.all_to_all(
        jnp.concatenate([w_gate, w_up], axis=2), CHIP, 0, 0, tiled=True
    ).reshape(HALF, -1)
    down_w = lax.all_to_all(w_down, CHIP, 0, 0, tiled=True).reshape(HALF, -1)

    piece = packed[:, : keys.shape[0]].reshape(-1, HD)
    near = [piece, across_y(piece), across_x(piece), across_xy(piece)]
    far = [swapped(p) for p in near]
    wo_near = packed[:, keys.shape[0] :]
    wo_far = swapped(wo_near)

    attended = attend(
        span_order,
        jnp.stack([ctx, exp % 2]).astype(jnp.int32),
        queries,
        near[0:2] + far[0:2],
        near[2:4] + far[2:4],
    )
    partner = across_y(attended)
    rows = jnp.stack(
        [attended.reshape(8, -1, 4 * HD), partner.reshape(8, -1, 4 * HD)], axis=1
    ).reshape(-1, 4, HD)

    def projected(w):
        w = w.reshape(8, 4, 64, HD)
        out = jnp.einsum("rhd,zhfd->rzf", rows, w, preferred_element_type=jnp.float32)
        return out.reshape(-1, HALF // 2)

    a, b = projected(wo_near), projected(wo_far)
    mixed = jnp.concatenate(
        [jnp.where(core == 0, a, b), jnp.where(core == 0, b, a)], axis=1
    ).astype(jnp.bfloat16)
    mixed = mixed.reshape(8, 32, HALF)
    summed = lax.dynamic_index_in_dim(mixed, exp, 0, False).astype(jnp.float32)
    for d in range(1, 8):
        sent = lax.dynamic_index_in_dim(mixed, exp ^ d, 0, False)
        got = lax.ppermute(sent, "exp", [(e, e ^ d) for e in range(8)])
        summed = summed + got.astype(jnp.float32)
    got = across_y(summed[16:])
    low = jnp.where(yh == 0, summed[:16], got).reshape(16, 2, 1, -1)
    high = jnp.where(yh == 0, got, summed[:16]).reshape(16, 2, 1, -1)
    summed = jnp.concatenate([low, high], axis=2).reshape(16, D)
    resid = by_plane(stream_in.astype(jnp.float32)) + summed
    gain = by_plane(norm_gain.astype(jnp.float32)[None])
    normed = (
        resid
        * lax.rsqrt(jnp.mean(resid * resid, axis=-1, keepdims=True) + 1e-06)
        * gain
    ).astype(jnp.bfloat16)

    rows = stream_in.shape[0]
    flat = expert_ids.reshape(-1)
    hits = (flat[:, None] == jnp.arange(EXPERTS, dtype=jnp.int32)[None, :]).astype(jnp.float32)
    before = (
        jnp.arange(rows * TOPK)[:, None] > jnp.arange(rows * TOPK)[None, :]
    ).astype(jnp.float32)
    ahead = jnp.dot(before, hits, preferred_element_type=jnp.float32)
    rank = jnp.sum(ahead * hits, axis=1).astype(jnp.int32)
    slots = (((flat % OWN) * 8 + flat // OWN) * CAP + rank).reshape(rows, TOPK)
    slot_ids = jnp.arange(EXPERTS * CAP, dtype=jnp.int32)
    placing = jnp.any(slots[None, :, :] == slot_ids[:, None, None], axis=2).astype(jnp.bfloat16)
    combine = jnp.sum(
        jnp.where(
            slots[:, :, None] == slot_ids[None, None, :],
            expert_gates[:, :, None],
            jnp.zeros((), jnp.bfloat16),
        ),
        axis=1,
    )

    outgoing = jnp.dot(placing, normed, preferred_element_type=jnp.float32).astype(jnp.bfloat16)
    outgoing = (
        outgoing.reshape(OWN, 8, CAP, 2, HALF)
        .transpose(0, 3, 1, 2, 4)
        .reshape(256, CAP, HALF)
    )
    tokens = lax.all_to_all(outgoing, ALL, 0, 0, tiled=True).reshape(512, HALF)

    gu = jnp.dot(tokens, gate_up_w, preferred_element_type=jnp.float32)
    gu = gu.reshape(2, 256, -1)
    keep = jnp.where(core == 0, gu[0], gu[1])
    send = jnp.where(core == 0, gu[1], gu[0])
    both = keep + swapped(send)
    width = both.shape[1] // 2
    act = (jax.nn.silu(both[:, :width]) * both[:, width:]).astype(jnp.bfloat16)
    act_other = swapped(act)
    act = jnp.concatenate(
        [jnp.where(core == 0, act, act_other), jnp.where(core == 0, act_other, act)],
        axis=0,
    )
    out = lax.dot_general(
        act, down_w, (((1,), (1,)), ((), ())), preferred_element_type=jnp.float32
    ).astype(jnp.bfloat16)
    home = lax.all_to_all(out.reshape(256, CAP, HALF), ALL, 0, 0, tiled=True)
    home = home.reshape(OWN, 2, 8, CAP, HALF).transpose(0, 2, 3, 1, 4).reshape(EXPERTS * CAP, D)
    moe = jnp.dot(combine, home, preferred_element_type=jnp.float32)
    return from_planes(resid + moe)


def solution(mesh):
    finer = Mesh(mesh.devices.reshape(2, 8, 2, 8), ALL)
    return jax.shard_map(
        shards,
        mesh=finer,
        in_specs=(
            P(CTX, "exp"),
            P(CTX, None),
            P(CTX, None),
            P(),
            P(ALL, None),
            P("exp", None, CTX),
            P(),
            P(ALL, None),
            P(ALL, None),
            P("exp", CTX, None),
            P("exp", CTX, None),
            P("exp", CTX, None),
        ),
        out_specs=P(ALL, None),
        check_vma=False,
    )
```

```python
import math

import jax
import jax.numpy as jnp
from jax import lax
from jax.experimental import pallas as pl
from jax.experimental.pallas import tpu as pltpu
from jax.sharding import Mesh
from jax.sharding import PartitionSpec as P


D = 2048
HALF = D // 2
HD = 128
TOPK = 8
SPAN = 64
EXPERTS = 128
OWN = 16
FF = 768
CAP = 2
CHIP = ("yh", "z")
CTX = ("yh", "z", "core")
ALL = ("yh", "z", "core", "exp")
NEG_BIG = -1e30
SWAP = [(0, 1), (1, 0)]


def swapped(x):
    return lax.ppermute(x, "core", SWAP)


def attend_pieces(span_ref, ctx, q_ref, keys, values, o_ref, s_ref):
    rows = q_ref.shape[0]
    part = keys[0].shape[0]
    blocks = part // 128
    yh = ctx // 16
    core = lax.rem(ctx, 2)
    q = q_ref[...]
    row = lax.broadcasted_iota(jnp.int32, (rows, 1), 0)
    q_place = jnp.where(
        row < SPAN,
        span_ref[2 * ctx] * SPAN + row,
        span_ref[2 * ctx + 1] * SPAN + row - SPAN,
    )
    lane = lax.broadcasted_iota(jnp.int32, (1, 2 * SPAN), 1)
    dims = (((1,), (1,)), ((), ()))
    top = jnp.full((rows, 128), NEG_BIG, jnp.float32)
    for side in range(4):
        first = (yh if side % 2 == 0 else 1 - yh) * 16 + (core if side < 2 else 1 - core)
        for b in range(blocks):
            k = keys[side][b * 128 : (b + 1) * 128, :]
            s = lax.dot_general(q, k, dims, preferred_element_type=jnp.float32)
            at = 2 * (first + 2 * b)
            place = jnp.where(
                lane < SPAN,
                span_ref[at] * SPAN + lane,
                span_ref[at + 1] * SPAN + lane - SPAN,
            )
            s = jnp.where(place <= q_place, s, NEG_BIG)
            c0 = (side * blocks + b) * 128
            s_ref[:, c0 : c0 + 128] = s
            top = jnp.maximum(top, s)
    top = jnp.max(top, axis=1, keepdims=True)
    scale = math.log2(math.e) / math.sqrt(HD)
    total = jnp.zeros((rows, 128), jnp.float32)
    acc = jnp.zeros((rows, HD), jnp.float32)
    wide = 512
    for side in range(4):
        for b in range(part // wide):
            c0 = side * part + b * wide
            p = jnp.exp2((s_ref[:, c0 : c0 + wide] - top) * scale)
            for j in range(wide // 128):
                total = total + p[:, j * 128 : (j + 1) * 128]
            v = values[side][b * wide : (b + 1) * wide, :]
            acc = acc + jnp.dot(p.astype(jnp.bfloat16), v, preferred_element_type=jnp.float32)
    o_ref[...] = (acc / jnp.sum(total, axis=1, keepdims=True)).astype(o_ref.dtype)


def attend_kernel(span_ref, where_ref, q_ref, *refs):
    own, cross = refs[0:4], refs[4:8]
    o_ref, s_ref = refs[8:]
    ctx = where_ref[0]

    @pl.when(where_ref[1] == 0)
    def _():
        attend_pieces(span_ref, ctx, q_ref, own, cross, o_ref, s_ref)

    @pl.when(where_ref[1] != 0)
    def _():
        attend_pieces(span_ref, ctx, q_ref, cross, own, o_ref, s_ref)


def attend(span_order, where, queries, own, cross):
    rows, width = queries.shape
    keys = 4 * own[0].shape[0]
    return pl.pallas_call(
        attend_kernel,
        out_shape=jax.ShapeDtypeStruct((rows, width), jnp.bfloat16),
        grid_spec=pltpu.PrefetchScalarGridSpec(
            num_scalar_prefetch=2,
            grid=(width // HD,),
            in_specs=[pl.BlockSpec((rows, HD), lambda h, *_: (0, h))]
            + [pl.BlockSpec(own[0].shape, lambda h, *_: (0, 0))] * 8,
            out_specs=pl.BlockSpec((rows, HD), lambda h, *_: (0, h)),
            scratch_shapes=[pltpu.VMEM((rows, keys), jnp.float32)],
        ),
        cost_estimate=pl.CostEstimate(
            flops=4 * rows * width * keys,
            bytes_accessed=4 * keys * HD + 4 * rows * width,
            transcendentals=rows * keys * width // HD,
        ),
    )(span_order, where, queries, *own, *cross)


def assemble_kernel(z_ref, *refs):
    parts, (piece_ref, wo_ref) = refs[:8], refs[8:]
    for r, part in enumerate(parts):
        at = lax.rem(z_ref[0] + r, 8)
        piece_ref[pl.ds(pl.multiple_of(at * HD, HD), HD), :] = part[0:HD, :]
        for h in range(4):
            wo_ref[pl.ds(pl.multiple_of(at * 64, 64), 64), h * HD : (h + 1) * HD] = part[
                HD + h * 64 : HD + (h + 1) * 64, :
            ]


def assembled(z, parts):
    return pl.pallas_call(
        assemble_kernel,
        out_shape=(
            jax.ShapeDtypeStruct((8 * HD, HD), jnp.bfloat16),
            jax.ShapeDtypeStruct((8 * 64, 4 * HD), jnp.bfloat16),
        ),
        grid_spec=pltpu.PrefetchScalarGridSpec(
            num_scalar_prefetch=1,
            grid=(1,),
            in_specs=[pl.BlockSpec(parts[0].shape, lambda i, *_: (0, 0))] * 8,
            out_specs=(
                pl.BlockSpec((8 * HD, HD), lambda i, *_: (0, 0)),
                pl.BlockSpec((8 * 64, 4 * HD), lambda i, *_: (0, 0)),
            ),
        ),
        cost_estimate=pl.CostEstimate(flops=0, bytes_accessed=1572864, transcendentals=0),
    )(z[None].astype(jnp.int32), *parts)


def across_y(x):
    return lax.ppermute(x, "yh", SWAP)


def across_x(x):
    return lax.ppermute(x, "exp", [(e, e ^ 1) for e in range(8)])


def across_xy(x):
    pairs = [(y * 8 + e, (1 - y) * 8 + (e ^ 1)) for y in range(2) for e in range(8)]
    return lax.ppermute(x, ("yh", "exp"), pairs)


def by_plane(x):
    rows = x.shape[0]
    return x.reshape(rows, D // 128, 2, 64).transpose(0, 2, 1, 3).reshape(rows, D)


def from_planes(x):
    rows = x.shape[0]
    return x.reshape(rows, 2, D // 128, 64).transpose(0, 2, 1, 3).reshape(rows, D)


def shards(
    queries,
    keys,
    values,
    span_order,
    stream_in,
    wo,
    norm_gain,
    expert_ids,
    expert_gates,
    w_gate,
    w_up,
    w_down,
):
    core = lax.axis_index("core")
    ctx = lax.axis_index(CTX)
    exp = lax.axis_index("exp")
    yh = lax.axis_index("yh")

    head = exp // 2 * HD
    mine = jnp.where(
        exp % 2 == 0,
        lax.dynamic_slice_in_dim(keys, head, HD, 1),
        lax.dynamic_slice_in_dim(values, head, HD, 1),
    )
    packed = jnp.concatenate([mine, wo.transpose(0, 2, 1).reshape(-1, HD)], axis=0)
    parts = [packed] + [
        lax.ppermute(packed, "z", [((i + r) % 8, i) for i in range(8)])
        for r in range(1, 8)
    ]
    weights = lax.all_to_all(
        jnp.concatenate([w_gate, w_up, w_down], axis=2), CHIP, 0, 0, tiled=True
    ).reshape(HALF, -1)
    gate_up_w, down_w = weights[:, : 2 * FF], weights[:, 2 * FF :]

    piece, wo_near = assembled(lax.axis_index("z"), parts)
    near = [piece, across_y(piece), across_x(piece), across_xy(piece)]
    far = [swapped(p) for p in near]
    wo_far = swapped(wo_near)

    attended = attend(
        span_order,
        jnp.stack([ctx, exp % 2]).astype(jnp.int32),
        queries,
        near[0:2] + far[0:2],
        near[2:4] + far[2:4],
    )
    partner = across_y(attended)
    rows = jnp.stack(
        [attended.reshape(8, -1, 4 * HD), partner.reshape(8, -1, 4 * HD)], axis=1
    ).reshape(-1, 4 * HD)

    def projected(w):
        return lax.dot_general(
            rows, w, (((1,), (1,)), ((), ())), preferred_element_type=jnp.float32
        )

    a, b = projected(wo_near), projected(wo_far)
    mixed = jnp.concatenate(
        [jnp.where(core == 0, a, b), jnp.where(core == 0, b, a)], axis=1
    ).astype(jnp.bfloat16)
    mixed = mixed.reshape(8, 32, HALF)
    summed = lax.dynamic_index_in_dim(mixed, exp, 0, False).astype(jnp.float32)
    for d in range(1, 8):
        sent = lax.dynamic_index_in_dim(mixed, exp ^ d, 0, False)
        got = lax.ppermute(sent, "exp", [(e, e ^ d) for e in range(8)])
        summed = summed + got.astype(jnp.float32)
    got = across_y(summed[16:])
    low = jnp.where(yh == 0, summed[:16], got).reshape(16, 2, 1, -1)
    high = jnp.where(yh == 0, got, summed[:16]).reshape(16, 2, 1, -1)
    summed = jnp.concatenate([low, high], axis=2).reshape(16, D)
    resid = by_plane(stream_in.astype(jnp.float32)) + summed
    gain = by_plane(norm_gain.astype(jnp.float32)[None])
    normed = (
        resid
        * lax.rsqrt(jnp.mean(resid * resid, axis=-1, keepdims=True) + 1e-06)
        * gain
    ).astype(jnp.bfloat16)

    rows = stream_in.shape[0]
    flat = expert_ids.reshape(-1)
    hits = (flat[:, None] == jnp.arange(EXPERTS, dtype=jnp.int32)[None, :]).astype(jnp.float32)
    before = (
        jnp.arange(rows * TOPK)[:, None] > jnp.arange(rows * TOPK)[None, :]
    ).astype(jnp.float32)
    ahead = jnp.dot(before, hits, preferred_element_type=jnp.float32)
    rank = jnp.sum(ahead * hits, axis=1).astype(jnp.int32)
    slots = (((flat % OWN) * 8 + flat // OWN) * CAP + rank).reshape(rows, TOPK)
    slot_ids = jnp.arange(EXPERTS * CAP, dtype=jnp.int32)
    placing = jnp.any(slots[None, :, :] == slot_ids[:, None, None], axis=2).astype(jnp.bfloat16)
    combine = jnp.sum(
        jnp.where(
            slots[:, :, None] == slot_ids[None, None, :],
            expert_gates[:, :, None],
            jnp.zeros((), jnp.bfloat16),
        ),
        axis=1,
    )

    outgoing = jnp.dot(placing, normed, preferred_element_type=jnp.float32).astype(jnp.bfloat16)
    outgoing = (
        outgoing.reshape(OWN, 8, CAP, 2, HALF)
        .transpose(0, 3, 1, 2, 4)
        .reshape(256, CAP, HALF)
    )
    tokens = lax.all_to_all(outgoing, ALL, 0, 0, tiled=True).reshape(512, HALF)

    gu = jnp.dot(tokens, gate_up_w, preferred_element_type=jnp.float32)
    gu = gu.reshape(2, 256, -1)
    keep = jnp.where(core == 0, gu[0], gu[1])
    send = jnp.where(core == 0, gu[1], gu[0])
    both = keep + swapped(send)
    width = both.shape[1] // 2
    act = (jax.nn.silu(both[:, :width]) * both[:, width:]).astype(jnp.bfloat16)
    act_other = swapped(act)
    act = jnp.concatenate(
        [jnp.where(core == 0, act, act_other), jnp.where(core == 0, act_other, act)],
        axis=0,
    )
    out = lax.dot_general(
        act, down_w, (((1,), (1,)), ((), ())), preferred_element_type=jnp.float32
    ).astype(jnp.bfloat16)
    home = lax.all_to_all(out.reshape(256, CAP, HALF), ALL, 0, 0, tiled=True)
    home = home.reshape(OWN, 2, 8, CAP, HALF).transpose(0, 2, 3, 1, 4).reshape(EXPERTS * CAP, D)
    moe = jnp.dot(combine, home, preferred_element_type=jnp.float32)
    return from_planes(resid + moe)


def solution(mesh):
    finer = Mesh(mesh.devices.reshape(2, 8, 2, 8), ALL)
    return jax.shard_map(
        shards,
        mesh=finer,
        in_specs=(
            P(CTX, "exp"),
            P(CTX, None),
            P(CTX, None),
            P(),
            P(ALL, None),
            P("exp", None, CTX),
            P(),
            P(ALL, None),
            P(ALL, None),
            P("exp", CTX, None),
            P("exp", CTX, None),
            P("exp", CTX, None),
        ),
        out_specs=P(ALL, None),
        check_vma=False,
    )
```

```python
import math

import jax
import jax.numpy as jnp
from jax import lax
from jax.experimental import pallas as pl
from jax.experimental.pallas import tpu as pltpu
from jax.sharding import Mesh
from jax.sharding import PartitionSpec as P


D = 2048
HALF = D // 2
HD = 128
TOPK = 8
SPAN = 64
EXPERTS = 128
OWN = 16
FF = 768
CAP = 2
CHIP = ("yh", "z")
CTX = ("yh", "z", "core")
ALL = ("yh", "z", "core", "exp")
NEG_BIG = -1e30
DOWN_STEPS = [(dy, r) for r in (4, 3, 5, 2, 6, 1, 7, 0) for dy in (0, 1) if (dy, r) != (0, 0)]
SWAP = [(0, 1), (1, 0)]


def swapped(x):
    return lax.ppermute(x, "core", SWAP)


def attend_kernel(span_ref, where_ref, q_ref, *refs):
    own, cross = refs[0:4], refs[4:8]
    o_ref, k_ref, v_ref, s_ref = refs[8:]
    ctx = where_ref[0]
    rows = q_ref.shape[0]
    part = own[0].shape[0]

    def fill(keys, values):
        for side in range(4):
            k_ref[side * part : (side + 1) * part, :] = keys[side][...]
            v_ref[side * part : (side + 1) * part, :] = values[side][...]

    @pl.when((pl.program_id(0) == 0) & (where_ref[1] == 0))
    def _():
        fill(own, cross)

    @pl.when((pl.program_id(0) == 0) & (where_ref[1] != 0))
    def _():
        fill(cross, own)

    blocks = part // 128
    yh = ctx // 16
    core = lax.rem(ctx, 2)
    q = q_ref[...]
    row = lax.broadcasted_iota(jnp.int32, (rows, 1), 0)
    q_place = jnp.where(
        row < SPAN,
        span_ref[2 * ctx] * SPAN + row,
        span_ref[2 * ctx + 1] * SPAN + row - SPAN,
    )
    lane = lax.broadcasted_iota(jnp.int32, (1, 2 * SPAN), 1)
    dims = (((1,), (1,)), ((), ()))
    top = jnp.full((rows, 128), NEG_BIG, jnp.float32)
    for side in range(4):
        first = (yh if side % 2 == 0 else 1 - yh) * 16 + (core if side < 2 else 1 - core)
        for b in range(blocks):
            c0 = (side * blocks + b) * 128
            k = k_ref[c0 : c0 + 128, :]
            s = lax.dot_general(q, k, dims, preferred_element_type=jnp.float32)
            at = 2 * (first + 2 * b)
            place = jnp.where(
                lane < SPAN,
                span_ref[at] * SPAN + lane,
                span_ref[at + 1] * SPAN + lane - SPAN,
            )
            s = jnp.where(place <= q_place, s, NEG_BIG)
            s_ref[:, c0 : c0 + 128] = s
            top = jnp.maximum(top, s)
    top = jnp.max(top, axis=1, keepdims=True)
    scale = math.log2(math.e) / math.sqrt(HD)
    total = jnp.zeros((rows, 128), jnp.float32)
    acc = jnp.zeros((rows, HD), jnp.float32)
    wide = 512
    for c0 in range(0, 4 * part, wide):
        p = jnp.exp2((s_ref[:, c0 : c0 + wide] - top) * scale)
        for j in range(wide // 128):
            total = total + p[:, j * 128 : (j + 1) * 128]
        v = v_ref[c0 : c0 + wide, :]
        acc = acc + jnp.dot(p.astype(jnp.bfloat16), v, preferred_element_type=jnp.float32)
    o_ref[...] = (acc / jnp.sum(total, axis=1, keepdims=True)).astype(o_ref.dtype)


def attend(span_order, where, queries, own, cross):
    rows, width = queries.shape
    keys = 4 * own[0].shape[0]
    return pl.pallas_call(
        attend_kernel,
        out_shape=jax.ShapeDtypeStruct((rows, width), jnp.bfloat16),
        grid_spec=pltpu.PrefetchScalarGridSpec(
            num_scalar_prefetch=2,
            grid=(width // HD,),
            in_specs=[pl.BlockSpec((rows, HD), lambda h, *_: (0, h))]
            + [pl.BlockSpec(own[0].shape, lambda h, *_: (0, 0))] * 8,
            out_specs=pl.BlockSpec((rows, HD), lambda h, *_: (0, h)),
            scratch_shapes=[
                pltpu.VMEM((keys, HD), jnp.bfloat16),
                pltpu.VMEM((keys, HD), jnp.bfloat16),
                pltpu.VMEM((rows, keys), jnp.float32),
            ],
        ),
        cost_estimate=pl.CostEstimate(
            flops=4 * rows * width * keys,
            bytes_accessed=4 * keys * HD + 4 * rows * width,
            transcendentals=rows * keys * width // HD,
        ),
    )(span_order, where, queries, *own, *cross)


def assemble_kernel(z_ref, *refs):
    parts, (piece_ref, wo_ref) = refs[:8], refs[8:]
    for r, part in enumerate(parts):
        at = lax.rem(z_ref[0] + r, 8)
        piece_ref[pl.ds(pl.multiple_of(at * HD, HD), HD), :] = part[0:HD, :]
        for h in range(4):
            wo_ref[pl.ds(pl.multiple_of(at * 64, 64), 64), h * HD : (h + 1) * HD] = part[
                HD + h * 64 : HD + (h + 1) * 64, :
            ]


def assembled(z, parts):
    return pl.pallas_call(
        assemble_kernel,
        out_shape=(
            jax.ShapeDtypeStruct((8 * HD, HD), jnp.bfloat16),
            jax.ShapeDtypeStruct((8 * 64, 4 * HD), jnp.bfloat16),
        ),
        grid_spec=pltpu.PrefetchScalarGridSpec(
            num_scalar_prefetch=1,
            grid=(1,),
            in_specs=[pl.BlockSpec(parts[0].shape, lambda i, *_: (0, 0))] * 8,
            out_specs=(
                pl.BlockSpec((8 * HD, HD), lambda i, *_: (0, 0)),
                pl.BlockSpec((8 * 64, 4 * HD), lambda i, *_: (0, 0)),
            ),
        ),
        cost_estimate=pl.CostEstimate(flops=0, bytes_accessed=1572864, transcendentals=0),
    )(z[None].astype(jnp.int32), *parts)


def project_kernel(ctx_ref, x_ref, *refs):
    weights, o_ref = refs[:4], refs[4]
    yh, core = ctx_ref[0] // 16, lax.rem(ctx_ref[0], 2)
    x = x_ref[...]
    for side, w in enumerate(weights):
        half = yh if side % 2 == 0 else 1 - yh
        plane = core if side < 2 else 1 - core
        out = lax.dot_general(
            x, w[...], (((1,), (1,)), ((), ())), preferred_element_type=jnp.float32
        )
        at = pl.multiple_of((2 * plane + half) * 512, 512)
        o_ref[:, pl.ds(at, 512)] = out.astype(o_ref.dtype)


def project(ctx, x, weights):
    return pl.pallas_call(
        project_kernel,
        out_shape=jax.ShapeDtypeStruct((x.shape[0], D), jnp.bfloat16),
        grid_spec=pltpu.PrefetchScalarGridSpec(
            num_scalar_prefetch=1,
            grid=(1,),
            in_specs=[pl.BlockSpec(a.shape, lambda i, *_: (0, 0)) for a in [x, *weights]],
            out_specs=pl.BlockSpec((x.shape[0], D), lambda i, *_: (0, 0)),
        ),
        cost_estimate=pl.CostEstimate(
            flops=2 * x.shape[0] * x.shape[1] * D, bytes_accessed=2752512, transcendentals=0
        ),
    )(ctx[None].astype(jnp.int32), x, *weights)


def down_kernel(ctx_ref, mine_ref, other_ref, *refs):
    pieces, (o_ref, w_ref) = refs[:16], refs[16:]
    yh, z, core = ctx_ref[0] // 16, lax.rem(ctx_ref[0], 16) // 2, lax.rem(ctx_ref[0], 2)
    for (dy, r), piece in zip([(0, 0)] + DOWN_STEPS, pieces):
        source = lax.rem(yh + dy, 2) * 8 + lax.rem(z + r, 8)
        w_ref[pl.ds(pl.multiple_of(source * 64, 64), 64), :] = piece[...]
    for act_ref, half in ((mine_ref, core), (other_ref, 1 - core)):
        out = lax.dot_general(
            act_ref[...], w_ref[...], (((1,), (1,)), ((), ())), preferred_element_type=jnp.float32
        )
        o_ref[pl.ds(pl.multiple_of(half * 256, 256), 256), :] = out.astype(o_ref.dtype)


def project_down(ctx, mine, other, pieces):
    arrays = [mine, other, *pieces]
    return pl.pallas_call(
        down_kernel,
        out_shape=jax.ShapeDtypeStruct((512, HALF), jnp.bfloat16),
        grid_spec=pltpu.PrefetchScalarGridSpec(
            num_scalar_prefetch=1,
            grid=(1,),
            in_specs=[pl.BlockSpec(a.shape, lambda i, *_: (0, 0)) for a in arrays],
            out_specs=pl.BlockSpec((512, HALF), lambda i, *_: (0, 0)),
            scratch_shapes=[pltpu.VMEM((HALF, FF), jnp.bfloat16)],
        ),
        cost_estimate=pl.CostEstimate(
            flops=2 * 512 * HALF * FF, bytes_accessed=3407872, transcendentals=0
        ),
    )(ctx[None].astype(jnp.int32), *arrays)


def across_y(x):
    return lax.ppermute(x, "yh", SWAP)


def across_x(x):
    return lax.ppermute(x, "exp", [(e, e ^ 1) for e in range(8)])


def across_xy(x):
    pairs = [(y * 8 + e, (1 - y) * 8 + (e ^ 1)) for y in range(2) for e in range(8)]
    return lax.ppermute(x, ("yh", "exp"), pairs)


def by_plane(x):
    rows = x.shape[0]
    return x.reshape(rows, D // 128, 2, 64).transpose(0, 2, 1, 3).reshape(rows, D)


def from_planes(x):
    rows = x.shape[0]
    return x.reshape(rows, 2, D // 128, 64).transpose(0, 2, 1, 3).reshape(rows, D)


def shards(
    queries,
    keys,
    values,
    span_order,
    stream_in,
    wo,
    norm_gain,
    expert_ids,
    expert_gates,
    w_gate,
    w_up,
    w_down,
):
    core = lax.axis_index("core")
    ctx = lax.axis_index(CTX)
    exp = lax.axis_index("exp")
    yh = lax.axis_index("yh")

    head = exp // 2 * HD
    mine = jnp.where(
        exp % 2 == 0,
        lax.dynamic_slice_in_dim(keys, head, HD, 1),
        lax.dynamic_slice_in_dim(values, head, HD, 1),
    )
    packed = jnp.concatenate([mine, wo.transpose(0, 2, 1).reshape(-1, HD)], axis=0)
    parts = [packed] + [
        lax.ppermute(packed, "z", [((i + r) % 8, i) for i in range(8)])
        for r in range(1, 8)
    ]
    gate_up_w = lax.all_to_all(
        jnp.concatenate([w_gate, w_up], axis=2), CHIP, 0, 0, tiled=True
    ).reshape(HALF, -1)

    piece, wo_near = assembled(lax.axis_index("z"), parts)
    near = [piece, across_y(piece), across_x(piece), across_xy(piece)]
    wo_near = [wo_near, across_y(wo_near)]
    far = [swapped(p) for p in near]
    wo_far = [swapped(w) for w in wo_near]

    down = [lax.dynamic_index_in_dim(w_down, yh * 8 + lax.axis_index("z"), 0, False)]
    for dy, r in DOWN_STEPS:
        to = (yh + dy) % 2 * 8 + (lax.axis_index("z") + 8 - r) % 8
        sent = lax.dynamic_index_in_dim(w_down, to, 0, False)
        pairs = [(y * 8 + z, (y + dy) % 2 * 8 + (z - r) % 8) for y in range(2) for z in range(8)]
        down.append(lax.ppermute(sent, CHIP, pairs))

    attended = attend(
        span_order,
        jnp.stack([ctx, exp % 2]).astype(jnp.int32),
        queries,
        near[0:2] + far[0:2],
        near[2:4] + far[2:4],
    )
    mixed = project(ctx, attended, wo_near + wo_far).reshape(8, 16, D)
    summed = lax.dynamic_index_in_dim(mixed, exp, 0, False).astype(jnp.float32)
    for d in range(1, 8):
        sent = lax.dynamic_index_in_dim(mixed, exp ^ d, 0, False)
        got = lax.ppermute(sent, "exp", [(e, e ^ d) for e in range(8)])
        summed = summed + got.astype(jnp.float32)
    resid = by_plane(stream_in.astype(jnp.float32)) + summed
    gain = by_plane(norm_gain.astype(jnp.float32)[None])
    normed = (
        resid
        * lax.rsqrt(jnp.mean(resid * resid, axis=-1, keepdims=True) + 1e-06)
        * gain
    ).astype(jnp.bfloat16)

    rows = stream_in.shape[0]
    flat = expert_ids.reshape(-1)
    hits = (flat[:, None] == jnp.arange(EXPERTS, dtype=jnp.int32)[None, :]).astype(jnp.float32)
    before = (
        jnp.arange(rows * TOPK)[:, None] > jnp.arange(rows * TOPK)[None, :]
    ).astype(jnp.float32)
    ahead = jnp.dot(before, hits, preferred_element_type=jnp.float32)
    rank = jnp.sum(ahead * hits, axis=1).astype(jnp.int32)
    slots = (((flat % OWN) * 8 + flat // OWN) * CAP + rank).reshape(rows, TOPK)
    slot_ids = jnp.arange(EXPERTS * CAP, dtype=jnp.int32)
    placing = jnp.any(slots[None, :, :] == slot_ids[:, None, None], axis=2).astype(jnp.bfloat16)
    combine = jnp.sum(
        jnp.where(
            slots[:, :, None] == slot_ids[None, None, :],
            expert_gates[:, :, None],
            jnp.zeros((), jnp.bfloat16),
        ),
        axis=1,
    )

    outgoing = jnp.dot(placing, normed, preferred_element_type=jnp.float32).astype(jnp.bfloat16)
    outgoing = (
        outgoing.reshape(OWN, 8, CAP, 2, HALF)
        .transpose(0, 3, 1, 2, 4)
        .reshape(256, CAP, HALF)
    )
    tokens = lax.all_to_all(outgoing, ALL, 0, 0, tiled=True).reshape(512, HALF)

    send = lax.dynamic_slice_in_dim(tokens, (1 - core) * 256, 256, 0)
    keep = lax.dynamic_slice_in_dim(tokens, core * 256, 256, 0)
    send = jnp.dot(send, gate_up_w, preferred_element_type=jnp.float32)
    got = swapped(send.astype(jnp.bfloat16))
    both = jnp.dot(keep, gate_up_w, preferred_element_type=jnp.float32)
    both, got = lax.optimization_barrier((both, got))
    both = both + got.astype(jnp.float32)
    act = (jax.nn.silu(both[:, :FF]) * both[:, FF:]).astype(jnp.bfloat16)
    act_other = swapped(act)
    out = project_down(ctx, act, act_other, down)
    home = lax.all_to_all(out.reshape(256, CAP, HALF), ALL, 0, 0, tiled=True)
    home = home.reshape(OWN, 2, 8, CAP, HALF).transpose(0, 2, 3, 1, 4).reshape(EXPERTS * CAP, D)
    moe = jnp.dot(combine, home, preferred_element_type=jnp.float32)
    return from_planes(resid + moe)


def solution(mesh):
    finer = Mesh(mesh.devices.reshape(2, 8, 2, 8), ALL)
    return jax.shard_map(
        shards,
        mesh=finer,
        in_specs=(
            P(CTX, "exp"),
            P(CTX, None),
            P(CTX, None),
            P(),
            P(ALL, None),
            P("exp", None, CTX),
            P(),
            P(ALL, None),
            P(ALL, None),
            P("exp", CTX, None),
            P("exp", CTX, None),
            P("exp", CTX, None),
        ),
        out_specs=P(ALL, None),
        check_vma=False,
    )
```

```python
import math

import jax
import jax.numpy as jnp
from jax import lax
from jax.experimental import pallas as pl
from jax.experimental.pallas import tpu as pltpu
from jax.sharding import Mesh
from jax.sharding import PartitionSpec as P


D = 2048
HALF = D // 2
HD = 128
TOPK = 8
SPAN = 64
EXPERTS = 128
OWN = 16
FF = 768
CAP = 2
CHIP = ("yh", "z")
CTX = ("yh", "z", "core")
ALL = ("yh", "z", "core", "exp")
NEG_BIG = -1e30
SWAP = [(0, 1), (1, 0)]


def swapped(x):
    return lax.ppermute(x, "core", SWAP)


def attend_kernel(span_ref, where_ref, q_ref, *refs):
    own, cross = refs[0:4], refs[4:8]
    o_ref, k_ref, v_ref, s_ref = refs[8:]
    ctx = where_ref[0]
    rows = q_ref.shape[0]
    part = own[0].shape[0]

    def fill(keys, values):
        for side in range(4):
            k_ref[side * part : (side + 1) * part, :] = keys[side][...]
            v_ref[side * part : (side + 1) * part, :] = values[side][...]

    @pl.when((pl.program_id(0) == 0) & (where_ref[1] == 0))
    def _():
        fill(own, cross)

    @pl.when((pl.program_id(0) == 0) & (where_ref[1] != 0))
    def _():
        fill(cross, own)

    blocks = part // 128
    yh = ctx // 16
    core = lax.rem(ctx, 2)
    q = q_ref[...]
    row = lax.broadcasted_iota(jnp.int32, (rows, 1), 0)
    q_place = jnp.where(
        row < SPAN,
        span_ref[2 * ctx] * SPAN + row,
        span_ref[2 * ctx + 1] * SPAN + row - SPAN,
    )
    lane = lax.broadcasted_iota(jnp.int32, (1, 2 * SPAN), 1)
    dims = (((1,), (1,)), ((), ()))

    def score(side, top):
        first = jnp.where(side % 2 == 0, yh, 1 - yh) * 16 + jnp.where(side < 2, core, 1 - core)
        for b in range(blocks):
            c0 = pl.multiple_of((side * blocks + b) * 128, 128)
            k = k_ref[pl.ds(c0, 128), :]
            s = lax.dot_general(q, k, dims, preferred_element_type=jnp.float32)
            at = 2 * (first + 2 * b)
            place = jnp.where(
                lane < SPAN,
                span_ref[at] * SPAN + lane,
                span_ref[at + 1] * SPAN + lane - SPAN,
            )
            s = jnp.where(place <= q_place, s, NEG_BIG)
            s_ref[:, pl.ds(c0, 128)] = s
            top = jnp.maximum(top, s)
        return top

    top = lax.fori_loop(0, 4, score, jnp.full((rows, 128), NEG_BIG, jnp.float32))
    top = jnp.max(top, axis=1, keepdims=True)
    scale = math.log2(math.e) / math.sqrt(HD)
    wide = 512

    def gather_values(side, state):
        total, acc = state
        for b in range(part // wide):
            c0 = pl.multiple_of(side * part + b * wide, wide)
            p = jnp.exp2((s_ref[:, pl.ds(c0, wide)] - top) * scale)
            for j in range(wide // 128):
                total = total + p[:, j * 128 : (j + 1) * 128]
            v = v_ref[pl.ds(c0, wide), :]
            acc = acc + jnp.dot(p.astype(jnp.bfloat16), v, preferred_element_type=jnp.float32)
        return total, acc

    total, acc = lax.fori_loop(
        0,
        4,
        gather_values,
        (jnp.zeros((rows, 128), jnp.float32), jnp.zeros((rows, HD), jnp.float32)),
    )
    o_ref[...] = (acc / jnp.sum(total, axis=1, keepdims=True)).astype(o_ref.dtype)


def attend(span_order, where, queries, own, cross):
    rows, width = queries.shape
    keys = 4 * own[0].shape[0]
    return pl.pallas_call(
        attend_kernel,
        out_shape=jax.ShapeDtypeStruct((rows, width), jnp.bfloat16),
        grid_spec=pltpu.PrefetchScalarGridSpec(
            num_scalar_prefetch=2,
            grid=(width // HD,),
            in_specs=[pl.BlockSpec((rows, HD), lambda h, *_: (0, h))]
            + [pl.BlockSpec(own[0].shape, lambda h, *_: (0, 0))] * 8,
            out_specs=pl.BlockSpec((rows, HD), lambda h, *_: (0, h)),
            scratch_shapes=[
                pltpu.VMEM((keys, HD), jnp.bfloat16),
                pltpu.VMEM((keys, HD), jnp.bfloat16),
                pltpu.VMEM((rows, keys), jnp.float32),
            ],
        ),
        cost_estimate=pl.CostEstimate(
            flops=4 * rows * width * keys,
            bytes_accessed=4 * keys * HD + 4 * rows * width,
            transcendentals=rows * keys * width // HD,
        ),
    )(span_order, where, queries, *own, *cross)


def assemble_kernel(z_ref, *refs):
    parts, (piece_ref, wo_ref) = refs[:8], refs[8:]
    for r, part in enumerate(parts):
        at = lax.rem(z_ref[0] + r, 8)
        piece_ref[pl.ds(pl.multiple_of(at * HD, HD), HD), :] = part[0:HD, :]
        for h in range(4):
            wo_ref[pl.ds(pl.multiple_of(at * 64, 64), 64), h * HD : (h + 1) * HD] = part[
                HD + h * 64 : HD + (h + 1) * 64, :
            ]


def assembled(z, parts):
    return pl.pallas_call(
        assemble_kernel,
        out_shape=(
            jax.ShapeDtypeStruct((8 * HD, HD), jnp.bfloat16),
            jax.ShapeDtypeStruct((8 * 64, 4 * HD), jnp.bfloat16),
        ),
        grid_spec=pltpu.PrefetchScalarGridSpec(
            num_scalar_prefetch=1,
            grid=(1,),
            in_specs=[pl.BlockSpec(parts[0].shape, lambda i, *_: (0, 0))] * 8,
            out_specs=(
                pl.BlockSpec((8 * HD, HD), lambda i, *_: (0, 0)),
                pl.BlockSpec((8 * 64, 4 * HD), lambda i, *_: (0, 0)),
            ),
        ),
        cost_estimate=pl.CostEstimate(flops=0, bytes_accessed=1572864, transcendentals=0),
    )(z[None].astype(jnp.int32), *parts)


def project_kernel(ctx_ref, x_ref, *refs):
    weights, o_ref = refs[:4], refs[4]
    yh, core = ctx_ref[0] // 16, lax.rem(ctx_ref[0], 2)
    x = x_ref[...]
    for side, w in enumerate(weights):
        half = yh if side % 2 == 0 else 1 - yh
        plane = core if side < 2 else 1 - core
        out = lax.dot_general(
            x, w[...], (((1,), (1,)), ((), ())), preferred_element_type=jnp.float32
        )
        at = pl.multiple_of((2 * plane + half) * 512, 512)
        o_ref[:, pl.ds(at, 512)] = out.astype(o_ref.dtype)


def project(ctx, x, weights):
    return pl.pallas_call(
        project_kernel,
        out_shape=jax.ShapeDtypeStruct((x.shape[0], D), jnp.bfloat16),
        grid_spec=pltpu.PrefetchScalarGridSpec(
            num_scalar_prefetch=1,
            grid=(1,),
            in_specs=[pl.BlockSpec(a.shape, lambda i, *_: (0, 0)) for a in [x, *weights]],
            out_specs=pl.BlockSpec((x.shape[0], D), lambda i, *_: (0, 0)),
        ),
        cost_estimate=pl.CostEstimate(
            flops=2 * x.shape[0] * x.shape[1] * D, bytes_accessed=2752512, transcendentals=0
        ),
    )(ctx[None].astype(jnp.int32), x, *weights)


def down_kernel(ctx_ref, *refs):
    pieces, w_ref = refs[:8], refs[8]
    yh, z = ctx_ref[0] // 16, lax.rem(ctx_ref[0], 16) // 2
    for r, piece in enumerate(pieces):
        for half, side in enumerate((yh, 1 - yh)):
            at = pl.multiple_of((side * 8 + lax.rem(z + r, 8)) * 64, 64)
            w_ref[pl.ds(at, 64), :] = piece[half * 64 : (half + 1) * 64, :]


def down_in_order(ctx, pieces):
    return pl.pallas_call(
        down_kernel,
        out_shape=jax.ShapeDtypeStruct((HALF, FF), jnp.bfloat16),
        grid_spec=pltpu.PrefetchScalarGridSpec(
            num_scalar_prefetch=1,
            grid=(1,),
            in_specs=[pl.BlockSpec(a.shape, lambda i, *_: (0, 0)) for a in pieces],
            out_specs=pl.BlockSpec((HALF, FF), lambda i, *_: (0, 0)),
        ),
        cost_estimate=pl.CostEstimate(flops=0, bytes_accessed=3145728, transcendentals=0),
    )(ctx[None].astype(jnp.int32), *pieces)


def across_y(x):
    return lax.ppermute(x, "yh", SWAP)


def across_x(x):
    return lax.ppermute(x, "exp", [(e, e ^ 1) for e in range(8)])


def across_xy(x):
    pairs = [(y * 8 + e, (1 - y) * 8 + (e ^ 1)) for y in range(2) for e in range(8)]
    return lax.ppermute(x, ("yh", "exp"), pairs)


def by_plane(x):
    rows = x.shape[0]
    return x.reshape(rows, D // 128, 2, 64).transpose(0, 2, 1, 3).reshape(rows, D)


def from_planes(x):
    rows = x.shape[0]
    return x.reshape(rows, 2, D // 128, 64).transpose(0, 2, 1, 3).reshape(rows, D)


def shards(
    queries,
    keys,
    values,
    span_order,
    stream_in,
    wo,
    norm_gain,
    expert_ids,
    expert_gates,
    w_gate,
    w_up,
    w_down,
):
    core = lax.axis_index("core")
    ctx = lax.axis_index(CTX)
    exp = lax.axis_index("exp")
    yh = lax.axis_index("yh")

    head = exp // 2 * HD
    mine = jnp.where(
        exp % 2 == 0,
        lax.dynamic_slice_in_dim(keys, head, HD, 1),
        lax.dynamic_slice_in_dim(values, head, HD, 1),
    )
    packed = jnp.concatenate([mine, wo.transpose(0, 2, 1).reshape(-1, HD)], axis=0)
    parts = [packed] + [
        lax.ppermute(packed, "z", [((i + r) % 8, i) for i in range(8)])
        for r in range(1, 8)
    ]
    gate_up_w = lax.all_to_all(
        jnp.concatenate([w_gate, w_up], axis=2), CHIP, 0, 0, tiled=True
    ).reshape(HALF, -1)

    piece, wo_near = assembled(lax.axis_index("z"), parts)
    near = [piece, across_y(piece), across_x(piece), across_xy(piece)]
    wo_near = [wo_near, across_y(wo_near)]
    far = [swapped(p) for p in near]
    wo_far = [swapped(w) for w in wo_near]
    here = lax.dynamic_slice_in_dim(w_down, yh * 8, 8, 0)
    there = across_y(lax.dynamic_slice_in_dim(w_down, (1 - yh) * 8, 8, 0))

    attended = attend(
        span_order,
        jnp.stack([ctx, exp % 2]).astype(jnp.int32),
        queries,
        near[0:2] + far[0:2],
        near[2:4] + far[2:4],
    )
    mixed = project(ctx, attended, wo_near + wo_far).reshape(8, 16, D)
    summed = lax.dynamic_index_in_dim(mixed, exp, 0, False).astype(jnp.float32)
    for d in range(1, 8):
        sent = lax.dynamic_index_in_dim(mixed, exp ^ d, 0, False)
        got = lax.ppermute(sent, "exp", [(e, e ^ d) for e in range(8)])
        summed = summed + got.astype(jnp.float32)
    z = lax.axis_index("z")
    down = []
    for r in range(8):
        to = (z + 8 - r) % 8
        both = jnp.concatenate(
            [lax.dynamic_index_in_dim(w, to, 0, False) for w in (here, there)], axis=0
        )
        if r:
            both = lax.ppermute(both, "z", [((i + r) % 8, i) for i in range(8)])
        down.append(both)
    resid = by_plane(stream_in.astype(jnp.float32)) + summed
    gain = by_plane(norm_gain.astype(jnp.float32)[None])
    normed = (
        resid
        * lax.rsqrt(jnp.mean(resid * resid, axis=-1, keepdims=True) + 1e-06)
        * gain
    ).astype(jnp.bfloat16)

    rows = stream_in.shape[0]
    flat = expert_ids.reshape(-1)
    hits = (flat[:, None] == jnp.arange(EXPERTS, dtype=jnp.int32)[None, :]).astype(jnp.float32)
    before = (
        jnp.arange(rows * TOPK)[:, None] > jnp.arange(rows * TOPK)[None, :]
    ).astype(jnp.float32)
    ahead = jnp.dot(before, hits, preferred_element_type=jnp.float32)
    rank = jnp.sum(ahead * hits, axis=1).astype(jnp.int32)
    slots = (((flat % OWN) * 8 + flat // OWN) * CAP + rank).reshape(rows, TOPK)
    slot_ids = jnp.arange(EXPERTS * CAP, dtype=jnp.int32)
    placing = jnp.any(slots[None, :, :] == slot_ids[:, None, None], axis=2).astype(jnp.bfloat16)
    combine = jnp.sum(
        jnp.where(
            slots[:, :, None] == slot_ids[None, None, :],
            expert_gates[:, :, None],
            jnp.zeros((), jnp.bfloat16),
        ),
        axis=1,
    )

    outgoing = jnp.dot(placing, normed, preferred_element_type=jnp.float32).astype(jnp.bfloat16)
    outgoing = (
        outgoing.reshape(OWN, 8, CAP, 2, HALF)
        .transpose(0, 3, 1, 2, 4)
        .reshape(256, CAP, HALF)
    )
    tokens = lax.all_to_all(outgoing, ALL, 0, 0, tiled=True).reshape(512, HALF)

    send = lax.dynamic_slice_in_dim(tokens, (1 - core) * 256, 256, 0)
    keep = lax.dynamic_slice_in_dim(tokens, core * 256, 256, 0)
    send = jnp.dot(send, gate_up_w, preferred_element_type=jnp.float32)
    got = swapped(send.astype(jnp.bfloat16))
    both = jnp.dot(keep, gate_up_w, preferred_element_type=jnp.float32)
    both, got = lax.optimization_barrier((both, got))
    both = both + got.astype(jnp.float32)
    act = (jax.nn.silu(both[:, :FF]) * both[:, FF:]).astype(jnp.bfloat16)
    act_other = swapped(act)
    act = jnp.concatenate(
        [jnp.where(core == 0, act, act_other), jnp.where(core == 0, act_other, act)],
        axis=0,
    )
    down_w = down_in_order(ctx, down)
    out = lax.dot_general(
        act, down_w, (((1,), (1,)), ((), ())), preferred_element_type=jnp.float32
    ).astype(jnp.bfloat16)
    home = lax.all_to_all(out.reshape(256, CAP, HALF), ALL, 0, 0, tiled=True)
    home = home.reshape(OWN, 2, 8, CAP, HALF).transpose(0, 2, 3, 1, 4).reshape(EXPERTS * CAP, D)
    moe = jnp.dot(combine, home, preferred_element_type=jnp.float32)
    return from_planes(resid + moe)


def solution(mesh):
    finer = Mesh(mesh.devices.reshape(2, 8, 2, 8), ALL)
    return jax.shard_map(
        shards,
        mesh=finer,
        in_specs=(
            P(CTX, "exp"),
            P(CTX, None),
            P(CTX, None),
            P(),
            P(ALL, None),
            P("exp", None, CTX),
            P(),
            P(ALL, None),
            P(ALL, None),
            P("exp", CTX, None),
            P("exp", CTX, None),
            P("exp", CTX, None),
        ),
        out_specs=P(ALL, None),
        check_vma=False,
    )
```

```python
import math

import jax
import jax.numpy as jnp
from jax import lax
from jax.experimental import pallas as pl
from jax.experimental.pallas import tpu as pltpu
from jax.sharding import Mesh
from jax.sharding import PartitionSpec as P


D = 2048
HALF = D // 2
HD = 128
TOPK = 8
SPAN = 64
EXPERTS = 128
OWN = 16
FF = 768
CAP = 2
CHIP = ("yh", "z")
CTX = ("yh", "z", "core")
ALL = ("yh", "z", "core", "exp")
NEG_BIG = -1e30
SWAP = [(0, 1), (1, 0)]


def swapped(x):
    return lax.ppermute(x, "core", SWAP)


def attend_pieces(span_ref, ctx, q_ref, keys, values, o_ref, s_ref):
    rows = q_ref.shape[0]
    part = keys[0].shape[0]
    blocks = part // 128
    yh = ctx // 16
    core = lax.rem(ctx, 2)
    q = q_ref[...]
    row = lax.broadcasted_iota(jnp.int32, (rows, 1), 0)
    q_place = jnp.where(
        row < SPAN,
        span_ref[2 * ctx] * SPAN + row,
        span_ref[2 * ctx + 1] * SPAN + row - SPAN,
    )
    lane = lax.broadcasted_iota(jnp.int32, (1, 2 * SPAN), 1)
    dims = (((1,), (1,)), ((), ()))
    top = jnp.full((rows, 128), NEG_BIG, jnp.float32)
    for side in range(4):
        first = (yh if side % 2 == 0 else 1 - yh) * 16 + (core if side < 2 else 1 - core)
        for b in range(blocks):
            k = keys[side][b * 128 : (b + 1) * 128, :]
            s = lax.dot_general(q, k, dims, preferred_element_type=jnp.float32)
            at = 2 * (first + 2 * b)
            place = jnp.where(
                lane < SPAN,
                span_ref[at] * SPAN + lane,
                span_ref[at + 1] * SPAN + lane - SPAN,
            )
            s = jnp.where(place <= q_place, s, NEG_BIG)
            c0 = (side * blocks + b) * 128
            s_ref[:, c0 : c0 + 128] = s
            top = jnp.maximum(top, s)
    top = jnp.max(top, axis=1, keepdims=True)
    scale = math.log2(math.e) / math.sqrt(HD)
    total = jnp.zeros((rows, 128), jnp.float32)
    acc = jnp.zeros((rows, HD), jnp.float32)
    wide = 512
    for side in range(4):
        for b in range(part // wide):
            c0 = side * part + b * wide
            p = jnp.exp2((s_ref[:, c0 : c0 + wide] - top) * scale)
            for j in range(wide // 128):
                total = total + p[:, j * 128 : (j + 1) * 128]
            v = values[side][b * wide : (b + 1) * wide, :]
            acc = acc + jnp.dot(p.astype(jnp.bfloat16), v, preferred_element_type=jnp.float32)
    o_ref[...] = (acc / jnp.sum(total, axis=1, keepdims=True)).astype(o_ref.dtype)


def attend_kernel(span_ref, where_ref, q_ref, *refs):
    own, cross = refs[0:4], refs[4:8]
    o_ref, s_ref = refs[8:]
    ctx = where_ref[0]

    @pl.when(where_ref[1] == 0)
    def _():
        attend_pieces(span_ref, ctx, q_ref, own, cross, o_ref, s_ref)

    @pl.when(where_ref[1] != 0)
    def _():
        attend_pieces(span_ref, ctx, q_ref, cross, own, o_ref, s_ref)


def attend(span_order, where, queries, own, cross):
    rows, width = queries.shape
    keys = 4 * own[0].shape[0]
    return pl.pallas_call(
        attend_kernel,
        out_shape=jax.ShapeDtypeStruct((rows, width), jnp.bfloat16),
        grid_spec=pltpu.PrefetchScalarGridSpec(
            num_scalar_prefetch=2,
            grid=(width // HD,),
            in_specs=[pl.BlockSpec((rows, HD), lambda h, *_: (0, h))]
            + [pl.BlockSpec(own[0].shape, lambda h, *_: (0, 0))] * 8,
            out_specs=pl.BlockSpec((rows, HD), lambda h, *_: (0, h)),
            scratch_shapes=[pltpu.VMEM((rows, keys), jnp.float32)],
        ),
        cost_estimate=pl.CostEstimate(
            flops=4 * rows * width * keys,
            bytes_accessed=4 * keys * HD + 4 * rows * width,
            transcendentals=rows * keys * width // HD,
        ),
    )(span_order, where, queries, *own, *cross)


def assemble_kernel(z_ref, *refs):
    parts, (piece_ref, wo_ref) = refs[:8], refs[8:]
    for r, part in enumerate(parts):
        at = lax.rem(z_ref[0] + r, 8)
        piece_ref[pl.ds(pl.multiple_of(at * HD, HD), HD), :] = part[0:HD, :]
        for h in range(4):
            wo_ref[pl.ds(pl.multiple_of(at * 64, 64), 64), h * HD : (h + 1) * HD] = part[
                HD + h * 64 : HD + (h + 1) * 64, :
            ]


def assembled(z, parts):
    return pl.pallas_call(
        assemble_kernel,
        out_shape=(
            jax.ShapeDtypeStruct((8 * HD, HD), jnp.bfloat16),
            jax.ShapeDtypeStruct((8 * 64, 4 * HD), jnp.bfloat16),
        ),
        grid_spec=pltpu.PrefetchScalarGridSpec(
            num_scalar_prefetch=1,
            grid=(1,),
            in_specs=[pl.BlockSpec(parts[0].shape, lambda i, *_: (0, 0))] * 8,
            out_specs=(
                pl.BlockSpec((8 * HD, HD), lambda i, *_: (0, 0)),
                pl.BlockSpec((8 * 64, 4 * HD), lambda i, *_: (0, 0)),
            ),
        ),
        cost_estimate=pl.CostEstimate(flops=0, bytes_accessed=1572864, transcendentals=0),
    )(z[None].astype(jnp.int32), *parts)


def project_kernel(ctx_ref, x_ref, *refs):
    weights, o_ref = refs[:4], refs[4]
    yh, core = ctx_ref[0] // 16, lax.rem(ctx_ref[0], 2)
    x = x_ref[...]
    for side, w in enumerate(weights):
        half = yh if side % 2 == 0 else 1 - yh
        plane = core if side < 2 else 1 - core
        out = lax.dot_general(
            x, w[...], (((1,), (1,)), ((), ())), preferred_element_type=jnp.float32
        )
        at = pl.multiple_of((2 * plane + half) * 512, 512)
        o_ref[:, pl.ds(at, 512)] = out.astype(o_ref.dtype)


def project(ctx, x, weights):
    return pl.pallas_call(
        project_kernel,
        out_shape=jax.ShapeDtypeStruct((x.shape[0], D), jnp.bfloat16),
        grid_spec=pltpu.PrefetchScalarGridSpec(
            num_scalar_prefetch=1,
            grid=(1,),
            in_specs=[pl.BlockSpec(a.shape, lambda i, *_: (0, 0)) for a in [x, *weights]],
            out_specs=pl.BlockSpec((x.shape[0], D), lambda i, *_: (0, 0)),
        ),
        cost_estimate=pl.CostEstimate(
            flops=2 * x.shape[0] * x.shape[1] * D, bytes_accessed=2752512, transcendentals=0
        ),
    )(ctx[None].astype(jnp.int32), x, *weights)


def across_y(x):
    return lax.ppermute(x, "yh", SWAP)


def across_x(x):
    return lax.ppermute(x, "exp", [(e, e ^ 1) for e in range(8)])


def across_xy(x):
    pairs = [(y * 8 + e, (1 - y) * 8 + (e ^ 1)) for y in range(2) for e in range(8)]
    return lax.ppermute(x, ("yh", "exp"), pairs)


def by_plane(x):
    rows = x.shape[0]
    return x.reshape(rows, D // 128, 2, 64).transpose(0, 2, 1, 3).reshape(rows, D)


def from_planes(x):
    rows = x.shape[0]
    return x.reshape(rows, 2, D // 128, 64).transpose(0, 2, 1, 3).reshape(rows, D)


def shards(
    queries,
    keys,
    values,
    span_order,
    stream_in,
    wo,
    norm_gain,
    expert_ids,
    expert_gates,
    w_gate,
    w_up,
    w_down,
):
    core = lax.axis_index("core")
    ctx = lax.axis_index(CTX)
    exp = lax.axis_index("exp")

    head = exp // 2 * HD
    mine = jnp.where(
        exp % 2 == 0,
        lax.dynamic_slice_in_dim(keys, head, HD, 1),
        lax.dynamic_slice_in_dim(values, head, HD, 1),
    )
    packed = jnp.concatenate([mine, wo.transpose(0, 2, 1).reshape(-1, HD)], axis=0)
    parts = [packed] + [
        lax.ppermute(packed, "z", [((i + r) % 8, i) for i in range(8)])
        for r in range(1, 8)
    ]
    weights = lax.all_to_all(
        jnp.concatenate([w_gate, w_up, w_down], axis=2), CHIP, 0, 0, tiled=True
    ).reshape(HALF, -1)

    piece, wo_near = assembled(lax.axis_index("z"), parts)
    near = [piece, across_y(piece), across_x(piece), across_xy(piece)]
    wo_near = [wo_near, across_y(wo_near)]
    far = [swapped(p) for p in near]
    wo_far = [swapped(w) for w in wo_near]

    attended = attend(
        span_order,
        jnp.stack([ctx, exp % 2]).astype(jnp.int32),
        queries,
        near[0:2] + far[0:2],
        near[2:4] + far[2:4],
    )
    mixed = project(ctx, attended, wo_near + wo_far).reshape(8, 16, D)
    summed = lax.dynamic_index_in_dim(mixed, exp, 0, False).astype(jnp.float32)
    for d in range(1, 8):
        sent = lax.dynamic_index_in_dim(mixed, exp ^ d, 0, False)
        got = lax.ppermute(sent, "exp", [(e, e ^ d) for e in range(8)])
        summed = summed + got.astype(jnp.float32)
    resid = by_plane(stream_in.astype(jnp.float32)) + summed
    gain = by_plane(norm_gain.astype(jnp.float32)[None])
    normed = (
        resid
        * lax.rsqrt(jnp.mean(resid * resid, axis=-1, keepdims=True) + 1e-06)
        * gain
    ).astype(jnp.bfloat16)

    rows = stream_in.shape[0]
    flat = expert_ids.reshape(-1)
    hits = (flat[:, None] == jnp.arange(EXPERTS, dtype=jnp.int32)[None, :]).astype(jnp.float32)
    before = (
        jnp.arange(rows * TOPK)[:, None] > jnp.arange(rows * TOPK)[None, :]
    ).astype(jnp.float32)
    ahead = jnp.dot(before, hits, preferred_element_type=jnp.float32)
    rank = jnp.sum(ahead * hits, axis=1).astype(jnp.int32)
    slots = (((flat % OWN) * 8 + flat // OWN) * CAP + rank).reshape(rows, TOPK)
    slot_ids = jnp.arange(EXPERTS * CAP, dtype=jnp.int32)
    placing = jnp.any(slots[None, :, :] == slot_ids[:, None, None], axis=2).astype(jnp.bfloat16)
    combine = jnp.sum(
        jnp.where(
            slots[:, :, None] == slot_ids[None, None, :],
            expert_gates[:, :, None],
            jnp.zeros((), jnp.bfloat16),
        ),
        axis=1,
    )

    outgoing = jnp.dot(placing, normed, preferred_element_type=jnp.float32).astype(jnp.bfloat16)
    outgoing = (
        outgoing.reshape(OWN, 8, CAP, 2, HALF)
        .transpose(0, 3, 1, 2, 4)
        .reshape(256, CAP, HALF)
    )
    tokens = lax.all_to_all(outgoing, ALL, 0, 0, tiled=True).reshape(512, HALF)

    half = FF // 2

    def columns(first, at):
        return lax.dynamic_slice_in_dim(weights, first + at * half, half, 1)

    def gate_up(at):
        return jnp.concatenate([columns(0, at), columns(FF, at)], axis=1)

    own_w = gate_up(core)
    other_w = swapped(gate_up(1 - core))
    own_down = columns(2 * FF, core)
    other_down = columns(2 * FF, 1 - core)
    tokens_other = swapped(tokens)
    hidden = jnp.dot(tokens, own_w, preferred_element_type=jnp.float32)
    hidden, tokens_other = lax.optimization_barrier((hidden, tokens_other))
    hidden = hidden + jnp.dot(tokens_other, other_w, preferred_element_type=jnp.float32)
    act = (jax.nn.silu(hidden[:, :half]) * hidden[:, half:]).astype(jnp.bfloat16)
    dims = (((1,), (1,)), ((), ()))
    act_other = swapped(act)
    out = lax.dot_general(act, own_down, dims, preferred_element_type=jnp.float32)
    out, act_other = lax.optimization_barrier((out, act_other))
    out = out + lax.dot_general(act_other, other_down, dims, preferred_element_type=jnp.float32)
    out = out.astype(jnp.bfloat16)
    home = lax.all_to_all(out.reshape(256, CAP, HALF), ALL, 0, 0, tiled=True)
    home = home.reshape(OWN, 2, 8, CAP, HALF).transpose(0, 2, 3, 1, 4).reshape(EXPERTS * CAP, D)
    moe = jnp.dot(combine, home, preferred_element_type=jnp.float32)
    return from_planes(resid + moe)


def solution(mesh):
    finer = Mesh(mesh.devices.reshape(2, 8, 2, 8), ALL)
    return jax.shard_map(
        shards,
        mesh=finer,
        in_specs=(
            P(CTX, "exp"),
            P(CTX, None),
            P(CTX, None),
            P(),
            P(ALL, None),
            P("exp", None, CTX),
            P(),
            P(ALL, None),
            P(ALL, None),
            P("exp", CTX, None),
            P("exp", CTX, None),
            P("exp", CTX, None),
        ),
        out_specs=P(ALL, None),
        check_vma=False,
    )
```

```python
import math

import jax
import jax.numpy as jnp
from jax import lax
from jax.experimental import pallas as pl
from jax.experimental.pallas import tpu as pltpu
from jax.sharding import Mesh
from jax.sharding import PartitionSpec as P


D = 2048
HALF = D // 2
HD = 128
TOPK = 8
SPAN = 64
EXPERTS = 128
OWN = 16
FF = 768
CAP = 2
CHIP = ("yh", "z")
CTX = ("yh", "z", "core")
ALL = ("yh", "z", "core", "exp")
NEG_BIG = -1e30
SWAP = [(0, 1), (1, 0)]


def swapped(x):
    return lax.ppermute(x, "core", SWAP)


def attend_pieces(span_ref, ctx, q_ref, keys, values, o_ref, s_ref):
    rows = q_ref.shape[0]
    part = keys[0].shape[0]
    blocks = part // 128
    q = q_ref[...]
    row = lax.broadcasted_iota(jnp.int32, (rows, 1), 0)
    q_place = jnp.where(
        row < SPAN,
        span_ref[2 * ctx] * SPAN + row,
        span_ref[2 * ctx + 1] * SPAN + row - SPAN,
    )
    lane = lax.broadcasted_iota(jnp.int32, (1, 2 * SPAN), 1)
    dims = (((1,), (1,)), ((), ()))
    top = jnp.full((rows, 128), NEG_BIG, jnp.float32)
    for side in range(4):
        for b in range(blocks):
            k = keys[side][b * 128 : (b + 1) * 128, :]
            s = lax.dot_general(q, k, dims, preferred_element_type=jnp.float32)
            plane, half, z = block_of(ctx, side, b)
            at = 2 * (half * 16 + z * 2 + plane)
            place = jnp.where(
                lane < SPAN,
                span_ref[at] * SPAN + lane,
                span_ref[at + 1] * SPAN + lane - SPAN,
            )
            s = jnp.where(place <= q_place, s, NEG_BIG)
            c0 = (side * blocks + b) * 128
            s_ref[:, c0 : c0 + 128] = s
            top = jnp.maximum(top, s)
    top = jnp.max(top, axis=1, keepdims=True)
    scale = math.log2(math.e) / math.sqrt(HD)
    total = jnp.zeros((rows, 128), jnp.float32)
    acc = jnp.zeros((rows, HD), jnp.float32)
    wide = 512
    for side in range(4):
        for b in range(part // wide):
            c0 = side * part + b * wide
            p = jnp.exp2((s_ref[:, c0 : c0 + wide] - top) * scale)
            for j in range(wide // 128):
                total = total + p[:, j * 128 : (j + 1) * 128]
            v = values[side][b * wide : (b + 1) * wide, :]
            acc = acc + jnp.dot(p.astype(jnp.bfloat16), v, preferred_element_type=jnp.float32)
    o_ref[...] = (acc / jnp.sum(total, axis=1, keepdims=True)).astype(o_ref.dtype)


def attend_kernel(span_ref, where_ref, q_ref, *refs):
    own, cross = refs[0:4], refs[4:8]
    o_ref, s_ref = refs[8:]
    ctx = where_ref[0]

    @pl.when(where_ref[1] == 0)
    def _():
        attend_pieces(span_ref, ctx, q_ref, own, cross, o_ref, s_ref)

    @pl.when(where_ref[1] != 0)
    def _():
        attend_pieces(span_ref, ctx, q_ref, cross, own, o_ref, s_ref)


def attend(span_order, where, queries, own, cross):
    rows, width = queries.shape
    keys = 4 * own[0].shape[0]
    return pl.pallas_call(
        attend_kernel,
        out_shape=jax.ShapeDtypeStruct((rows, width), jnp.bfloat16),
        grid_spec=pltpu.PrefetchScalarGridSpec(
            num_scalar_prefetch=2,
            grid=(width // HD,),
            in_specs=[pl.BlockSpec((rows, HD), lambda h, *_: (0, h))]
            + [pl.BlockSpec(own[0].shape, lambda h, *_: (0, 0))] * 8,
            out_specs=pl.BlockSpec((rows, HD), lambda h, *_: (0, h)),
            scratch_shapes=[pltpu.VMEM((rows, keys), jnp.float32)],
        ),
        cost_estimate=pl.CostEstimate(
            flops=4 * rows * width * keys,
            bytes_accessed=4 * keys * HD + 4 * rows * width,
            transcendentals=rows * keys * width // HD,
        ),
    )(span_order, where, queries, *own, *cross)


def assemble_kernel(*refs):
    parts, (piece_ref, wo_ref) = refs[:5], refs[5:]
    rows = 3 * HD
    at = 0
    for part in parts:
        for first in range(0, part.shape[0], rows):
            piece_ref[at * HD : (at + 1) * HD, :] = part[first : first + HD, :]
            for h in range(4):
                f = first + HD + h * 64
                wo_ref[at * 64 : (at + 1) * 64, h * HD : (h + 1) * HD] = part[f : f + 64, :]
            at += 1


def assembled(parts):
    return pl.pallas_call(
        assemble_kernel,
        out_shape=(
            jax.ShapeDtypeStruct((8 * HD, HD), jnp.bfloat16),
            jax.ShapeDtypeStruct((8 * 64, 4 * HD), jnp.bfloat16),
        ),
        in_specs=[pl.BlockSpec(memory_space=pltpu.VMEM)] * 5,
        out_specs=(pl.BlockSpec(memory_space=pltpu.VMEM),) * 2,
        cost_estimate=pl.CostEstimate(flops=0, bytes_accessed=1572864, transcendentals=0),
    )(*parts)


def block_of(ctx, side, b):
    yh, z, core = ctx // 16, lax.rem(ctx, 16) // 2, lax.rem(ctx, 2)
    half = yh if side % 2 == 0 else 1 - yh
    holder = core if side < 2 else 1 - core
    plane = holder if b in (0, 7) else (b - 1) % 2
    away = (0, 1, 1, 2, 2, 3, 3, 4)[b]
    return plane, half, lax.rem(z + 8 + away * (1 - 2 * holder), 8)


def project_kernel(ctx_ref, x_ref, *refs):
    weights, (o_ref, w_ref) = refs[:4], refs[4:]
    for side, w in enumerate(weights):
        for b in range(8):
            plane, half, z = block_of(ctx_ref[0], side, b)
            at = pl.multiple_of(plane * HALF + half * (HALF // 2) + z * 64, 64)
            w_ref[pl.ds(at, 64), :] = w[b * 64 : (b + 1) * 64, :]
    out = lax.dot_general(
        x_ref[...], w_ref[...], (((1,), (1,)), ((), ())), preferred_element_type=jnp.float32
    )
    o_ref[...] = out.astype(o_ref.dtype)


def project(ctx, x, weights):
    return pl.pallas_call(
        project_kernel,
        out_shape=jax.ShapeDtypeStruct((x.shape[0], D), jnp.bfloat16),
        grid_spec=pltpu.PrefetchScalarGridSpec(
            num_scalar_prefetch=1,
            grid=(1,),
            in_specs=[pl.BlockSpec(a.shape, lambda i, *_: (0, 0)) for a in [x, *weights]],
            out_specs=pl.BlockSpec((x.shape[0], D), lambda i, *_: (0, 0)),
            scratch_shapes=[pltpu.VMEM((D, x.shape[1]), jnp.bfloat16)],
        ),
        cost_estimate=pl.CostEstimate(
            flops=2 * x.shape[0] * x.shape[1] * D, bytes_accessed=2752512, transcendentals=0
        ),
    )(ctx[None].astype(jnp.int32), x, *weights)


def across_y(x):
    return lax.ppermute(x, "yh", SWAP)


def across_x(x):
    return lax.ppermute(x, "exp", [(e, e ^ 1) for e in range(8)])


def across_xy(x):
    pairs = [(y * 8 + e, (1 - y) * 8 + (e ^ 1)) for y in range(2) for e in range(8)]
    return lax.ppermute(x, ("yh", "exp"), pairs)


def by_plane(x):
    rows = x.shape[0]
    return x.reshape(rows, D // 128, 2, 64).transpose(0, 2, 1, 3).reshape(rows, D)


def from_planes(x):
    rows = x.shape[0]
    return x.reshape(rows, 2, D // 128, 64).transpose(0, 2, 1, 3).reshape(rows, D)


def shards(
    queries,
    keys,
    values,
    span_order,
    stream_in,
    wo,
    norm_gain,
    expert_ids,
    expert_gates,
    w_gate,
    w_up,
    w_down,
):
    core = lax.axis_index("core")
    ctx = lax.axis_index(CTX)
    exp = lax.axis_index("exp")

    head = exp // 2 * HD
    mine = jnp.where(
        exp % 2 == 0,
        lax.dynamic_slice_in_dim(keys, head, HD, 1),
        lax.dynamic_slice_in_dim(values, head, HD, 1),
    )
    packed = jnp.concatenate([mine, wo.transpose(0, 2, 1).reshape(-1, HD)], axis=0)
    other = swapped(packed)
    both = jnp.concatenate(
        [jnp.where(core == 0, packed, other), jnp.where(core == 0, other, packed)], axis=0
    )
    parts = [packed]
    for j in range(1, 4):
        pairs = [
            ((i + (j if c == 0 else 8 - j)) % 8 * 2 + c, i * 2 + c)
            for i in range(8)
            for c in range(2)
        ]
        parts.append(lax.ppermute(both, ("z", "core"), pairs))
    parts.append(lax.ppermute(packed, "z", [((i + 4) % 8, i) for i in range(8)]))
    weights = lax.all_to_all(
        jnp.concatenate([w_gate, w_up, w_down], axis=2), CHIP, 0, 0, tiled=True
    ).reshape(HALF, -1)

    piece, wo_near = assembled(parts)
    near = [piece, across_y(piece), across_x(piece), across_xy(piece)]
    wo_near = [wo_near, across_y(wo_near)]
    far = [swapped(p) for p in near]
    wo_far = [swapped(w) for w in wo_near]

    attended = attend(
        span_order,
        jnp.stack([ctx, exp % 2]).astype(jnp.int32),
        queries,
        near[0:2] + far[0:2],
        near[2:4] + far[2:4],
    )
    mixed = project(ctx, attended, wo_near + wo_far).reshape(8, 16, D)
    summed = lax.dynamic_index_in_dim(mixed, exp, 0, False).astype(jnp.float32)
    for d in range(1, 8):
        sent = lax.dynamic_index_in_dim(mixed, exp ^ d, 0, False)
        got = lax.ppermute(sent, "exp", [(e, e ^ d) for e in range(8)])
        summed = summed + got.astype(jnp.float32)
    resid = by_plane(stream_in.astype(jnp.float32)) + summed
    gain = by_plane(norm_gain.astype(jnp.float32)[None])
    normed = (
        resid
        * lax.rsqrt(jnp.mean(resid * resid, axis=-1, keepdims=True) + 1e-06)
        * gain
    ).astype(jnp.bfloat16)

    rows = stream_in.shape[0]
    flat = expert_ids.reshape(-1)
    hits = (flat[:, None] == jnp.arange(EXPERTS, dtype=jnp.int32)[None, :]).astype(jnp.float32)
    before = (
        jnp.arange(rows * TOPK)[:, None] > jnp.arange(rows * TOPK)[None, :]
    ).astype(jnp.float32)
    ahead = jnp.dot(before, hits, preferred_element_type=jnp.float32)
    rank = jnp.sum(ahead * hits, axis=1).astype(jnp.int32)
    slots = (((flat % OWN) * 8 + flat // OWN) * CAP + rank).reshape(rows, TOPK)
    slot_ids = jnp.arange(EXPERTS * CAP, dtype=jnp.int32)
    placing = jnp.any(slots[None, :, :] == slot_ids[:, None, None], axis=2).astype(jnp.bfloat16)
    combine = jnp.sum(
        jnp.where(
            slots[:, :, None] == slot_ids[None, None, :],
            expert_gates[:, :, None],
            jnp.zeros((), jnp.bfloat16),
        ),
        axis=1,
    )

    outgoing = jnp.dot(placing, normed, preferred_element_type=jnp.float32).astype(jnp.bfloat16)
    outgoing = (
        outgoing.reshape(OWN, 8, CAP, 2, HALF)
        .transpose(0, 3, 1, 2, 4)
        .reshape(256, CAP, HALF)
    )
    tokens = lax.all_to_all(outgoing, ALL, 0, 0, tiled=True).reshape(512, HALF)

    half = FF // 2

    def columns(first, at):
        return lax.dynamic_slice_in_dim(weights, first + at * half, half, 1)

    def gate_up(at):
        return jnp.concatenate([columns(0, at), columns(FF, at)], axis=1)

    own_w = gate_up(core)
    other_w = swapped(gate_up(1 - core))
    own_down = columns(2 * FF, core)
    other_down = columns(2 * FF, 1 - core)
    tokens_other = swapped(tokens)
    hidden = jnp.dot(tokens, own_w, preferred_element_type=jnp.float32)
    hidden, tokens_other = lax.optimization_barrier((hidden, tokens_other))
    hidden = hidden + jnp.dot(tokens_other, other_w, preferred_element_type=jnp.float32)
    act = (jax.nn.silu(hidden[:, :half]) * hidden[:, half:]).astype(jnp.bfloat16)
    dims = (((1,), (1,)), ((), ()))
    act_other = swapped(act)
    out = lax.dot_general(act, own_down, dims, preferred_element_type=jnp.float32)
    out, act_other = lax.optimization_barrier((out, act_other))
    out = out + lax.dot_general(act_other, other_down, dims, preferred_element_type=jnp.float32)
    out = out.astype(jnp.bfloat16)
    home = lax.all_to_all(out.reshape(256, CAP, HALF), ALL, 0, 0, tiled=True)
    home = home.reshape(OWN, 2, 8, CAP, HALF).transpose(0, 2, 3, 1, 4).reshape(EXPERTS * CAP, D)
    moe = jnp.dot(combine, home, preferred_element_type=jnp.float32)
    return from_planes(resid + moe)


def solution(mesh):
    finer = Mesh(mesh.devices.reshape(2, 8, 2, 8), ALL)
    return jax.shard_map(
        shards,
        mesh=finer,
        in_specs=(
            P(CTX, "exp"),
            P(CTX, None),
            P(CTX, None),
            P(),
            P(ALL, None),
            P("exp", None, CTX),
            P(),
            P(ALL, None),
            P(ALL, None),
            P("exp", CTX, None),
            P("exp", CTX, None),
            P("exp", CTX, None),
        ),
        out_specs=P(ALL, None),
        check_vma=False,
    )
```

```python
import math

import jax
import jax.numpy as jnp
from jax import lax
from jax.experimental import pallas as pl
from jax.experimental.pallas import tpu as pltpu
from jax.sharding import Mesh
from jax.sharding import PartitionSpec as P


D = 2048
HALF = D // 2
HD = 128
TOPK = 8
SPAN = 64
EXPERTS = 128
OWN = 16
FF = 768
CAP = 2
CHIP = ("yh", "z")
CTX = ("yh", "z", "core")
ALL = ("yh", "z", "core", "exp")
NEG_BIG = -1e30
SWAP = [(0, 1), (1, 0)]


def swapped(x):
    return lax.ppermute(x, "core", SWAP)


def attend_pieces(span_ref, ctx, q_ref, keys, values, o_ref, s_ref):
    rows = q_ref.shape[0]
    part = keys[0].shape[0]
    blocks = part // 128
    q = q_ref[...]
    row = lax.broadcasted_iota(jnp.int32, (rows, 1), 0)
    q_place = jnp.where(
        row < SPAN,
        span_ref[2 * ctx] * SPAN + row,
        span_ref[2 * ctx + 1] * SPAN + row - SPAN,
    )
    lane = lax.broadcasted_iota(jnp.int32, (1, 2 * SPAN), 1)
    dims = (((1,), (1,)), ((), ()))
    top = jnp.full((rows, 128), NEG_BIG, jnp.float32)
    for side in range(4):
        for b in range(blocks):
            k = keys[side][b * 128 : (b + 1) * 128, :]
            s = lax.dot_general(q, k, dims, preferred_element_type=jnp.float32)
            plane, half, z = block_of(ctx, side, b)
            at = 2 * (half * 16 + z * 2 + plane)
            place = jnp.where(
                lane < SPAN,
                span_ref[at] * SPAN + lane,
                span_ref[at + 1] * SPAN + lane - SPAN,
            )
            s = jnp.where(place <= q_place, s, NEG_BIG)
            c0 = (side * blocks + b) * 128
            s_ref[:, c0 : c0 + 128] = s
            top = jnp.maximum(top, s)
    top = jnp.max(top, axis=1, keepdims=True)
    scale = math.log2(math.e) / math.sqrt(HD)
    total = jnp.zeros((rows, 128), jnp.float32)
    acc = jnp.zeros((rows, HD), jnp.float32)
    wide = 512
    for side in range(4):
        for b in range(part // wide):
            c0 = side * part + b * wide
            p = jnp.exp2((s_ref[:, c0 : c0 + wide] - top) * scale)
            for j in range(wide // 128):
                total = total + p[:, j * 128 : (j + 1) * 128]
            v = values[side][b * wide : (b + 1) * wide, :]
            acc = acc + jnp.dot(p.astype(jnp.bfloat16), v, preferred_element_type=jnp.float32)
    o_ref[...] = (acc / jnp.sum(total, axis=1, keepdims=True)).astype(o_ref.dtype)


def attend_kernel(span_ref, where_ref, q_ref, *refs):
    own, cross = refs[0:4], refs[4:8]
    o_ref, s_ref = refs[8:]
    ctx = where_ref[0]

    @pl.when(where_ref[1] == 0)
    def _():
        attend_pieces(span_ref, ctx, q_ref, own, cross, o_ref, s_ref)

    @pl.when(where_ref[1] != 0)
    def _():
        attend_pieces(span_ref, ctx, q_ref, cross, own, o_ref, s_ref)


def attend(span_order, where, queries, own, cross):
    rows, width = queries.shape
    keys = 4 * own[0].shape[0]
    return pl.pallas_call(
        attend_kernel,
        out_shape=jax.ShapeDtypeStruct((rows, width), jnp.bfloat16),
        grid_spec=pltpu.PrefetchScalarGridSpec(
            num_scalar_prefetch=2,
            grid=(width // HD,),
            in_specs=[pl.BlockSpec((rows, HD), lambda h, *_: (0, h))]
            + [pl.BlockSpec(own[0].shape, lambda h, *_: (0, 0))] * 8,
            out_specs=pl.BlockSpec((rows, HD), lambda h, *_: (0, h)),
            scratch_shapes=[pltpu.VMEM((rows, keys), jnp.float32)],
        ),
        cost_estimate=pl.CostEstimate(
            flops=4 * rows * width * keys,
            bytes_accessed=4 * keys * HD + 4 * rows * width,
            transcendentals=rows * keys * width // HD,
        ),
    )(span_order, where, queries, *own, *cross)


def assemble_kernel(*refs):
    parts, (piece_ref, wo_ref) = refs[:5], refs[5:]
    rows = 3 * HD
    at = 0
    for part in parts:
        for first in range(0, part.shape[0], rows):
            piece_ref[at * HD : (at + 1) * HD, :] = part[first : first + HD, :]
            for h in range(4):
                f = first + HD + h * 64
                wo_ref[at * 64 : (at + 1) * 64, h * HD : (h + 1) * HD] = part[f : f + 64, :]
            at += 1


def assembled(parts):
    return pl.pallas_call(
        assemble_kernel,
        out_shape=(
            jax.ShapeDtypeStruct((8 * HD, HD), jnp.bfloat16),
            jax.ShapeDtypeStruct((8 * 64, 4 * HD), jnp.bfloat16),
        ),
        in_specs=[pl.BlockSpec(memory_space=pltpu.VMEM)] * 5,
        out_specs=(pl.BlockSpec(memory_space=pltpu.VMEM),) * 2,
        cost_estimate=pl.CostEstimate(flops=0, bytes_accessed=1572864, transcendentals=0),
    )(*parts)


def block_of(ctx, side, b):
    yh, z, core = ctx // 16, lax.rem(ctx, 16) // 2, lax.rem(ctx, 2)
    half = yh if side % 2 == 0 else 1 - yh
    holder = core if side < 2 else 1 - core
    plane = holder if b in (0, 7) else (b - 1) % 2
    away = (0, 1, 1, 2, 2, 3, 3, 4)[b]
    return plane, half, lax.rem(z + 8 + away * (1 - 2 * holder), 8)


def project_kernel(ctx_ref, x_ref, *refs):
    weights, (o_ref, w_ref) = refs[:4], refs[4:]
    for side, w in enumerate(weights):
        for b in range(8):
            plane, half, z = block_of(ctx_ref[0], side, b)
            at = pl.multiple_of(plane * HALF + half * (HALF // 2) + z * 64, 64)
            w_ref[pl.ds(at, 64), :] = w[b * 64 : (b + 1) * 64, :]
    out = lax.dot_general(
        x_ref[...], w_ref[...], (((1,), (1,)), ((), ())), preferred_element_type=jnp.float32
    )
    o_ref[...] = out.astype(o_ref.dtype)


def project(ctx, x, weights):
    return pl.pallas_call(
        project_kernel,
        out_shape=jax.ShapeDtypeStruct((x.shape[0], D), jnp.bfloat16),
        grid_spec=pltpu.PrefetchScalarGridSpec(
            num_scalar_prefetch=1,
            grid=(1,),
            in_specs=[pl.BlockSpec(a.shape, lambda i, *_: (0, 0)) for a in [x, *weights]],
            out_specs=pl.BlockSpec((x.shape[0], D), lambda i, *_: (0, 0)),
            scratch_shapes=[pltpu.VMEM((D, x.shape[1]), jnp.bfloat16)],
        ),
        cost_estimate=pl.CostEstimate(
            flops=2 * x.shape[0] * x.shape[1] * D, bytes_accessed=2752512, transcendentals=0
        ),
    )(ctx[None].astype(jnp.int32), x, *weights)


def place_kernel(exp_ref, *refs):
    blocks, (o_ref, row_ref) = refs[:8], refs[8:]
    for d, block in enumerate(blocks):
        row_ref[d * 16 : (d + 1) * 16, :] = block[...].astype(jnp.float32)
    exp = exp_ref[0]
    codes = jnp.transpose(row_ref[:, D:])
    slot = lax.broadcasted_iota(jnp.int32, (256, 128), 0)
    lane = lax.broadcasted_iota(jnp.int32, (256, 128), 1)
    wanted = ((exp * OWN + slot // 16) * CAP + slot % CAP).astype(jnp.float32)
    hit = jnp.zeros((256, 128), jnp.float32)
    for t in range(TOPK):
        hit = hit + jnp.where(codes[t : t + 1, :] == wanted, 1.0, 0.0)
    hit = jnp.where((slot % 16) // CAP == jnp.bitwise_xor(lane // 16, exp), hit, 0.0)
    hit = hit.astype(jnp.bfloat16)
    for plane in range(2):
        x = row_ref[:, plane * HALF : (plane + 1) * HALF].astype(jnp.bfloat16)
        out = jnp.dot(hit, x, preferred_element_type=jnp.float32).astype(o_ref.dtype)
        for k in range(OWN):
            o_ref[2 * k + plane, :, :] = out[k * 16 : (k + 1) * 16, :]


def placed(exp, blocks):
    return pl.pallas_call(
        place_kernel,
        out_shape=jax.ShapeDtypeStruct((2 * OWN, 16, HALF), jnp.bfloat16),
        grid_spec=pltpu.PrefetchScalarGridSpec(
            num_scalar_prefetch=1,
            grid=(1,),
            in_specs=[pl.BlockSpec(b.shape, lambda i, *_: (0, 0)) for b in blocks],
            out_specs=pl.BlockSpec((2 * OWN, 16, HALF), lambda i, *_: (0, 0, 0)),
            scratch_shapes=[pltpu.VMEM((128, D + 128), jnp.float32)],
        ),
        cost_estimate=pl.CostEstimate(
            flops=2 * 256 * 128 * D, bytes_accessed=1605632, transcendentals=0
        ),
    )(exp[None].astype(jnp.int32), *blocks)


def across_y(x):
    return lax.ppermute(x, "yh", SWAP)


def across_x(x):
    return lax.ppermute(x, "exp", [(e, e ^ 1) for e in range(8)])


def across_xy(x):
    pairs = [(y * 8 + e, (1 - y) * 8 + (e ^ 1)) for y in range(2) for e in range(8)]
    return lax.ppermute(x, ("yh", "exp"), pairs)


def by_plane(x):
    rows = x.shape[0]
    return x.reshape(rows, D // 128, 2, 64).transpose(0, 2, 1, 3).reshape(rows, D)


def from_planes(x):
    rows = x.shape[0]
    return x.reshape(rows, 2, D // 128, 64).transpose(0, 2, 1, 3).reshape(rows, D)


def shards(
    queries,
    keys,
    values,
    span_order,
    stream_in,
    wo,
    norm_gain,
    expert_ids,
    expert_gates,
    w_gate,
    w_up,
    w_down,
):
    core = lax.axis_index("core")
    ctx = lax.axis_index(CTX)
    exp = lax.axis_index("exp")

    head = exp // 2 * HD
    mine = jnp.where(
        exp % 2 == 0,
        lax.dynamic_slice_in_dim(keys, head, HD, 1),
        lax.dynamic_slice_in_dim(values, head, HD, 1),
    )
    packed = jnp.concatenate([mine, wo.transpose(0, 2, 1).reshape(-1, HD)], axis=0)
    other = swapped(packed)
    both = jnp.concatenate(
        [jnp.where(core == 0, packed, other), jnp.where(core == 0, other, packed)], axis=0
    )
    parts = [packed]
    for j in range(1, 4):
        pairs = [
            ((i + (j if c == 0 else 8 - j)) % 8 * 2 + c, i * 2 + c)
            for i in range(8)
            for c in range(2)
        ]
        parts.append(lax.ppermute(both, ("z", "core"), pairs))
    parts.append(lax.ppermute(packed, "z", [((i + 4) % 8, i) for i in range(8)]))
    weights = lax.all_to_all(
        jnp.concatenate([w_gate, w_up, w_down], axis=2), CHIP, 0, 0, tiled=True
    ).reshape(HALF, -1)

    piece, wo_near = assembled(parts)
    near = [piece, across_y(piece), across_x(piece), across_xy(piece)]
    wo_near = [wo_near, across_y(wo_near)]
    far = [swapped(p) for p in near]
    wo_far = [swapped(w) for w in wo_near]

    attended = attend(
        span_order,
        jnp.stack([ctx, exp % 2]).astype(jnp.int32),
        queries,
        near[0:2] + far[0:2],
        near[2:4] + far[2:4],
    )
    mixed = project(ctx, attended, wo_near + wo_far).reshape(8, 16, D)
    summed = lax.dynamic_index_in_dim(mixed, exp, 0, False).astype(jnp.float32)
    for d in range(1, 8):
        sent = lax.dynamic_index_in_dim(mixed, exp ^ d, 0, False)
        got = lax.ppermute(sent, "exp", [(e, e ^ d) for e in range(8)])
        summed = summed + got.astype(jnp.float32)
    resid = by_plane(stream_in.astype(jnp.float32)) + summed
    gain = by_plane(norm_gain.astype(jnp.float32)[None])
    normed = (
        resid
        * lax.rsqrt(jnp.mean(resid * resid, axis=-1, keepdims=True) + 1e-06)
        * gain
    ).astype(jnp.bfloat16)

    rows = stream_in.shape[0]
    flat = expert_ids.reshape(-1)
    hits = (flat[:, None] == jnp.arange(EXPERTS, dtype=jnp.int32)[None, :]).astype(jnp.float32)
    before = (
        jnp.arange(rows * TOPK)[:, None] > jnp.arange(rows * TOPK)[None, :]
    ).astype(jnp.float32)
    ahead = jnp.dot(before, hits, preferred_element_type=jnp.float32)
    rank = jnp.sum(ahead * hits, axis=1).astype(jnp.int32)
    slots = (((flat % OWN) * 8 + flat // OWN) * CAP + rank).reshape(rows, TOPK)
    slot_ids = jnp.arange(EXPERTS * CAP, dtype=jnp.int32)
    codes = (flat * CAP + rank).reshape(rows, TOPK).astype(jnp.bfloat16)
    codes = jnp.pad(codes, ((0, 0), (0, 128 - TOPK)))
    combine = jnp.sum(
        jnp.where(
            slots[:, :, None] == slot_ids[None, None, :],
            expert_gates[:, :, None],
            jnp.zeros((), jnp.bfloat16),
        ),
        axis=1,
    )

    payload = jnp.concatenate([normed, codes], axis=1)
    blocks = [payload] + [
        lax.ppermute(payload, "exp", [(e, e ^ d) for e in range(8)]) for d in range(1, 8)
    ]
    outgoing = placed(exp, blocks)
    tokens = lax.all_to_all(outgoing, CTX, 0, 0, tiled=True).reshape(512, HALF)

    half = FF // 2

    def columns(first, at):
        return lax.dynamic_slice_in_dim(weights, first + at * half, half, 1)

    def gate_up(at):
        return jnp.concatenate([columns(0, at), columns(FF, at)], axis=1)

    own_w = gate_up(core)
    other_w = swapped(gate_up(1 - core))
    own_down = columns(2 * FF, core)
    other_down = columns(2 * FF, 1 - core)
    tokens_other = swapped(tokens)
    hidden = jnp.dot(tokens, own_w, preferred_element_type=jnp.float32)
    hidden, tokens_other = lax.optimization_barrier((hidden, tokens_other))
    hidden = hidden + jnp.dot(tokens_other, other_w, preferred_element_type=jnp.float32)
    act = (jax.nn.silu(hidden[:, :half]) * hidden[:, half:]).astype(jnp.bfloat16)
    dims = (((1,), (1,)), ((), ()))
    act_other = swapped(act)
    out = lax.dot_general(act, own_down, dims, preferred_element_type=jnp.float32)
    out, act_other = lax.optimization_barrier((out, act_other))
    out = out + lax.dot_general(act_other, other_down, dims, preferred_element_type=jnp.float32)
    out = out.astype(jnp.bfloat16)
    home = lax.all_to_all(out.reshape(256, CAP, HALF), ALL, 0, 0, tiled=True)
    home = home.reshape(OWN, 2, 8, CAP, HALF).transpose(0, 2, 3, 1, 4).reshape(EXPERTS * CAP, D)
    moe = jnp.dot(combine, home, preferred_element_type=jnp.float32)
    return from_planes(resid + moe)


def solution(mesh):
    finer = Mesh(mesh.devices.reshape(2, 8, 2, 8), ALL)
    return jax.shard_map(
        shards,
        mesh=finer,
        in_specs=(
            P(CTX, "exp"),
            P(CTX, None),
            P(CTX, None),
            P(),
            P(ALL, None),
            P("exp", None, CTX),
            P(),
            P(ALL, None),
            P(ALL, None),
            P("exp", CTX, None),
            P("exp", CTX, None),
            P("exp", CTX, None),
        ),
        out_specs=P(ALL, None),
        check_vma=False,
    )
```

```python
import math

import jax
import jax.numpy as jnp
from jax import lax
from jax.experimental import pallas as pl
from jax.experimental.pallas import tpu as pltpu
from jax.sharding import Mesh
from jax.sharding import PartitionSpec as P


D = 2048
HALF = D // 2
HD = 128
TOPK = 8
SPAN = 64
EXPERTS = 128
OWN = 16
FF = 768
CAP = 2
CHIP = ("yh", "z")
CTX = ("yh", "z", "core")
ALL = ("yh", "z", "core", "exp")
NEG_BIG = -1e30
SWAP = [(0, 1), (1, 0)]


def swapped(x):
    return lax.ppermute(x, "core", SWAP)


def attend_pieces(span_ref, ctx, q_ref, keys, values, o_ref, s_ref):
    rows = q_ref.shape[0]
    part = keys[0].shape[0]
    blocks = part // 128
    q = q_ref[...]
    row = lax.broadcasted_iota(jnp.int32, (rows, 1), 0)
    q_place = jnp.where(
        row < SPAN,
        span_ref[2 * ctx] * SPAN + row,
        span_ref[2 * ctx + 1] * SPAN + row - SPAN,
    )
    lane = lax.broadcasted_iota(jnp.int32, (1, 2 * SPAN), 1)
    dims = (((1,), (1,)), ((), ()))
    top = jnp.full((rows, 128), NEG_BIG, jnp.float32)
    for side in range(4):
        for b in range(blocks):
            k = keys[side][b * 128 : (b + 1) * 128, :]
            s = lax.dot_general(q, k, dims, preferred_element_type=jnp.float32)
            plane, half, z = block_of(ctx, side, b)
            at = 2 * (half * 16 + z * 2 + plane)
            place = jnp.where(
                lane < SPAN,
                span_ref[at] * SPAN + lane,
                span_ref[at + 1] * SPAN + lane - SPAN,
            )
            s = jnp.where(place <= q_place, s, NEG_BIG)
            c0 = (side * blocks + b) * 128
            s_ref[:, c0 : c0 + 128] = s
            top = jnp.maximum(top, s)
    top = jnp.max(top, axis=1, keepdims=True)
    scale = math.log2(math.e) / math.sqrt(HD)
    total = jnp.zeros((rows, 128), jnp.float32)
    acc = jnp.zeros((rows, HD), jnp.float32)
    wide = 512
    for side in range(4):
        for b in range(part // wide):
            c0 = side * part + b * wide
            p = jnp.exp2((s_ref[:, c0 : c0 + wide] - top) * scale)
            for j in range(wide // 128):
                total = total + p[:, j * 128 : (j + 1) * 128]
            v = values[side][b * wide : (b + 1) * wide, :]
            acc = acc + jnp.dot(p.astype(jnp.bfloat16), v, preferred_element_type=jnp.float32)
    o_ref[...] = (acc / jnp.sum(total, axis=1, keepdims=True)).astype(o_ref.dtype)


def attend_kernel(span_ref, where_ref, q_ref, *refs):
    own, cross = refs[0:4], refs[4:8]
    o_ref, s_ref = refs[8:]
    ctx = where_ref[0]

    @pl.when(where_ref[1] == 0)
    def _():
        attend_pieces(span_ref, ctx, q_ref, own, cross, o_ref, s_ref)

    @pl.when(where_ref[1] != 0)
    def _():
        attend_pieces(span_ref, ctx, q_ref, cross, own, o_ref, s_ref)


def attend(span_order, where, queries, own, cross):
    rows, width = queries.shape
    keys = 4 * own[0].shape[0]
    return pl.pallas_call(
        attend_kernel,
        out_shape=jax.ShapeDtypeStruct((rows, width), jnp.bfloat16),
        grid_spec=pltpu.PrefetchScalarGridSpec(
            num_scalar_prefetch=2,
            grid=(width // HD,),
            in_specs=[pl.BlockSpec((rows, HD), lambda h, *_: (0, h))]
            + [pl.BlockSpec(own[0].shape, lambda h, *_: (0, 0))] * 8,
            out_specs=pl.BlockSpec((rows, HD), lambda h, *_: (0, h)),
            scratch_shapes=[pltpu.VMEM((rows, keys), jnp.float32)],
        ),
        cost_estimate=pl.CostEstimate(
            flops=4 * rows * width * keys,
            bytes_accessed=4 * keys * HD + 4 * rows * width,
            transcendentals=rows * keys * width // HD,
        ),
    )(span_order, where, queries, *own, *cross)


def assemble_kernel(*refs):
    parts, (piece_ref, wo_ref) = refs[:5], refs[5:]
    rows = 3 * HD
    at = 0
    for part in parts:
        for first in range(0, part.shape[0], rows):
            piece_ref[at * HD : (at + 1) * HD, :] = part[first : first + HD, :]
            for h in range(4):
                f = first + HD + h * 64
                wo_ref[at * 64 : (at + 1) * 64, h * HD : (h + 1) * HD] = part[f : f + 64, :]
            at += 1


def assembled(parts):
    return pl.pallas_call(
        assemble_kernel,
        out_shape=(
            jax.ShapeDtypeStruct((8 * HD, HD), jnp.bfloat16),
            jax.ShapeDtypeStruct((8 * 64, 4 * HD), jnp.bfloat16),
        ),
        in_specs=[pl.BlockSpec(memory_space=pltpu.VMEM)] * 5,
        out_specs=(pl.BlockSpec(memory_space=pltpu.VMEM),) * 2,
        cost_estimate=pl.CostEstimate(flops=0, bytes_accessed=1572864, transcendentals=0),
    )(*parts)


def block_of(ctx, side, b):
    yh, z, core = ctx // 16, lax.rem(ctx, 16) // 2, lax.rem(ctx, 2)
    half = yh if side % 2 == 0 else 1 - yh
    holder = core if side < 2 else 1 - core
    plane = holder if b in (0, 7) else (b - 1) % 2
    away = (0, 1, 1, 2, 2, 3, 3, 4)[b]
    return plane, half, lax.rem(z + 8 + away * (1 - 2 * holder), 8)


def project_kernel(ctx_ref, x_ref, *refs):
    weights, (o_ref, w_ref) = refs[:4], refs[4:]
    for side, w in enumerate(weights):
        for b in range(8):
            plane, half, z = block_of(ctx_ref[0], side, b)
            at = pl.multiple_of(plane * HALF + half * (HALF // 2) + z * 64, 64)
            w_ref[pl.ds(at, 64), :] = w[b * 64 : (b + 1) * 64, :]
    out = lax.dot_general(
        x_ref[...], w_ref[...], (((1,), (1,)), ((), ())), preferred_element_type=jnp.float32
    )
    o_ref[...] = out.astype(o_ref.dtype)


def project(ctx, x, weights):
    return pl.pallas_call(
        project_kernel,
        out_shape=jax.ShapeDtypeStruct((x.shape[0], D), jnp.bfloat16),
        grid_spec=pltpu.PrefetchScalarGridSpec(
            num_scalar_prefetch=1,
            grid=(1,),
            in_specs=[pl.BlockSpec(a.shape, lambda i, *_: (0, 0)) for a in [x, *weights]],
            out_specs=pl.BlockSpec((x.shape[0], D), lambda i, *_: (0, 0)),
            scratch_shapes=[pltpu.VMEM((D, x.shape[1]), jnp.bfloat16)],
        ),
        cost_estimate=pl.CostEstimate(
            flops=2 * x.shape[0] * x.shape[1] * D, bytes_accessed=2752512, transcendentals=0
        ),
    )(ctx[None].astype(jnp.int32), x, *weights)


def place_kernel(exp_ref, *refs):
    blocks, (o_ref, row_ref) = refs[:8], refs[8:]
    for d, block in enumerate(blocks):
        row_ref[d * 16 : (d + 1) * 16, :] = block[...].astype(jnp.float32)
    exp = exp_ref[0]
    codes = jnp.transpose(row_ref[:, D:])
    slot = lax.broadcasted_iota(jnp.int32, (256, 128), 0)
    lane = lax.broadcasted_iota(jnp.int32, (256, 128), 1)
    wanted = ((exp * OWN + slot // 16) * CAP + slot % CAP).astype(jnp.float32)
    hit = jnp.zeros((256, 128), jnp.float32)
    for t in range(TOPK):
        hit = hit + jnp.where(codes[t : t + 1, :] == wanted, 1.0, 0.0)
    hit = jnp.where((slot % 16) // CAP == jnp.bitwise_xor(lane // 16, exp), hit, 0.0)
    hit = hit.astype(jnp.bfloat16)
    for plane in range(2):
        x = row_ref[:, plane * HALF : (plane + 1) * HALF].astype(jnp.bfloat16)
        out = jnp.dot(hit, x, preferred_element_type=jnp.float32).astype(o_ref.dtype)
        for k in range(OWN):
            o_ref[2 * k + plane, :, :] = out[k * 16 : (k + 1) * 16, :]


def placed(exp, blocks):
    return pl.pallas_call(
        place_kernel,
        out_shape=jax.ShapeDtypeStruct((2 * OWN, 16, HALF), jnp.bfloat16),
        grid_spec=pltpu.PrefetchScalarGridSpec(
            num_scalar_prefetch=1,
            grid=(1,),
            in_specs=[pl.BlockSpec(b.shape, lambda i, *_: (0, 0)) for b in blocks],
            out_specs=pl.BlockSpec((2 * OWN, 16, HALF), lambda i, *_: (0, 0, 0)),
            scratch_shapes=[pltpu.VMEM((128, D + 128), jnp.float32)],
        ),
        cost_estimate=pl.CostEstimate(
            flops=2 * 256 * 128 * D, bytes_accessed=1605632, transcendentals=0
        ),
    )(exp[None].astype(jnp.int32), *blocks)


def down_kernel(act_ref, act_other_ref, own_ref, other_ref, o_ref):
    dims = (((1,), (1,)), ((), ()))
    out = lax.dot_general(act_ref[...], own_ref[...], dims, preferred_element_type=jnp.float32)
    out = out + lax.dot_general(
        act_other_ref[...], other_ref[...], dims, preferred_element_type=jnp.float32
    )
    o_ref[...] = out.astype(o_ref.dtype).reshape(o_ref.shape)


def project_down(act, act_other, own, other):
    slots, half = act.shape
    step = slots // 4
    rows = pl.BlockSpec((step, half), lambda i: (i, 0))
    whole = pl.BlockSpec(own.shape, lambda i: (0, 0))
    return pl.pallas_call(
        down_kernel,
        out_shape=jax.ShapeDtypeStruct((slots // CAP, CAP, HALF), jnp.bfloat16),
        grid=(4,),
        in_specs=[rows, rows, whole, whole],
        out_specs=pl.BlockSpec((step // CAP, CAP, HALF), lambda i: (i, 0, 0)),
        cost_estimate=pl.CostEstimate(
            flops=4 * slots * half * HALF, bytes_accessed=3407872, transcendentals=0
        ),
    )(act, act_other, own, other)


def combine_kernel(gates_ref, home_ref, low_ref, high_ref, o_ref):
    wide = low_ref.shape[1]
    planes = []
    for plane, resid_ref in enumerate((low_ref, high_ref)):
        x = jnp.concatenate(
            [
                home_ref[(2 * k + plane) * 8 : (2 * k + plane + 1) * 8, :, :].reshape(16, wide)
                for k in range(OWN)
            ],
            axis=0,
        )
        moe = jnp.dot(gates_ref[...], x, preferred_element_type=jnp.float32)
        planes.append(resid_ref[...] + moe)
    lane = lax.broadcasted_iota(jnp.int32, (16, 128), 1)
    for j in range(wide // 128):
        low = planes[0][:, j * 128 : (j + 1) * 128]
        high = planes[1][:, j * 128 : (j + 1) * 128]
        o_ref[:, 2 * j * 128 : (2 * j + 1) * 128] = jnp.where(
            lane < 64, low, pltpu.roll(high, 64, 1)
        )
        o_ref[:, (2 * j + 1) * 128 : (2 * j + 2) * 128] = jnp.where(
            lane < 64, pltpu.roll(low, 64, 1), high
        )


def combined(gates, home, resid):
    rows = resid.shape[0]
    return pl.pallas_call(
        combine_kernel,
        out_shape=jax.ShapeDtypeStruct(resid.shape, jnp.float32),
        grid=(4,),
        in_specs=[
            pl.BlockSpec(gates.shape, lambda i: (0, 0)),
            pl.BlockSpec((256, CAP, HALF // 4), lambda i: (0, 0, i)),
            pl.BlockSpec((rows, HALF // 4), lambda i: (0, i)),
            pl.BlockSpec((rows, HALF // 4), lambda i: (0, i + 4)),
        ],
        out_specs=pl.BlockSpec((rows, HALF // 2), lambda i: (0, i)),
        cost_estimate=pl.CostEstimate(
            flops=2 * 16 * 512 * HALF, bytes_accessed=1318912, transcendentals=0
        ),
    )(gates, home, resid, resid)


def across_y(x):
    return lax.ppermute(x, "yh", SWAP)


def across_x(x):
    return lax.ppermute(x, "exp", [(e, e ^ 1) for e in range(8)])


def across_xy(x):
    pairs = [(y * 8 + e, (1 - y) * 8 + (e ^ 1)) for y in range(2) for e in range(8)]
    return lax.ppermute(x, ("yh", "exp"), pairs)


def by_plane(x):
    rows = x.shape[0]
    return x.reshape(rows, D // 128, 2, 64).transpose(0, 2, 1, 3).reshape(rows, D)


def shards(
    queries,
    keys,
    values,
    span_order,
    stream_in,
    wo,
    norm_gain,
    expert_ids,
    expert_gates,
    w_gate,
    w_up,
    w_down,
):
    core = lax.axis_index("core")
    ctx = lax.axis_index(CTX)
    exp = lax.axis_index("exp")

    head = exp // 2 * HD
    mine = jnp.where(
        exp % 2 == 0,
        lax.dynamic_slice_in_dim(keys, head, HD, 1),
        lax.dynamic_slice_in_dim(values, head, HD, 1),
    )
    packed = jnp.concatenate([mine, wo.transpose(0, 2, 1).reshape(-1, HD)], axis=0)
    other = swapped(packed)
    both = jnp.concatenate(
        [jnp.where(core == 0, packed, other), jnp.where(core == 0, other, packed)], axis=0
    )
    parts = [packed]
    for j in range(1, 4):
        pairs = [
            ((i + (j if c == 0 else 8 - j)) % 8 * 2 + c, i * 2 + c)
            for i in range(8)
            for c in range(2)
        ]
        parts.append(lax.ppermute(both, ("z", "core"), pairs))
    parts.append(lax.ppermute(packed, "z", [((i + 4) % 8, i) for i in range(8)]))
    weights = lax.all_to_all(
        jnp.concatenate([w_gate, w_up, w_down], axis=2), CHIP, 0, 0, tiled=True
    ).reshape(HALF, -1)

    piece, wo_near = assembled(parts)
    near = [piece, across_y(piece), across_x(piece), across_xy(piece)]
    wo_near = [wo_near, across_y(wo_near)]
    far = [swapped(p) for p in near]
    wo_far = [swapped(w) for w in wo_near]

    attended = attend(
        span_order,
        jnp.stack([ctx, exp % 2]).astype(jnp.int32),
        queries,
        near[0:2] + far[0:2],
        near[2:4] + far[2:4],
    )
    mixed = project(ctx, attended, wo_near + wo_far).reshape(8, 16, D)
    summed = lax.dynamic_index_in_dim(mixed, exp, 0, False).astype(jnp.float32)
    for d in range(1, 8):
        sent = lax.dynamic_index_in_dim(mixed, exp ^ d, 0, False)
        got = lax.ppermute(sent, "exp", [(e, e ^ d) for e in range(8)])
        summed = summed + got.astype(jnp.float32)
    resid = by_plane(stream_in.astype(jnp.float32)) + summed
    gain = by_plane(norm_gain.astype(jnp.float32)[None])
    normed = (
        resid
        * lax.rsqrt(jnp.mean(resid * resid, axis=-1, keepdims=True) + 1e-06)
        * gain
    ).astype(jnp.bfloat16)

    rows = stream_in.shape[0]
    flat = expert_ids.reshape(-1)
    hits = (flat[:, None] == jnp.arange(EXPERTS, dtype=jnp.int32)[None, :]).astype(jnp.float32)
    before = (
        jnp.arange(rows * TOPK)[:, None] > jnp.arange(rows * TOPK)[None, :]
    ).astype(jnp.float32)
    ahead = jnp.dot(before, hits, preferred_element_type=jnp.float32)
    rank = jnp.sum(ahead * hits, axis=1).astype(jnp.int32)
    slots = (((flat % OWN) * 8 + flat // OWN) * CAP + rank).reshape(rows, TOPK)
    slot_ids = jnp.arange(EXPERTS * CAP, dtype=jnp.int32)
    codes = (flat * CAP + rank).reshape(rows, TOPK).astype(jnp.bfloat16)
    codes = jnp.pad(codes, ((0, 0), (0, 128 - TOPK)))
    combine = jnp.sum(
        jnp.where(
            slots[:, :, None] == slot_ids[None, None, :],
            expert_gates[:, :, None],
            jnp.zeros((), jnp.bfloat16),
        ),
        axis=1,
    )

    payload = jnp.concatenate([normed, codes], axis=1)
    blocks = [payload] + [
        lax.ppermute(payload, "exp", [(e, e ^ d) for e in range(8)]) for d in range(1, 8)
    ]
    outgoing = placed(exp, blocks)
    tokens = lax.all_to_all(outgoing, CTX, 0, 0, tiled=True).reshape(512, HALF)

    half = FF // 2

    def columns(first, at):
        return lax.dynamic_slice_in_dim(weights, first + at * half, half, 1)

    def gate_up(at):
        return jnp.concatenate([columns(0, at), columns(FF, at)], axis=1)

    own_w = gate_up(core)
    other_w = swapped(gate_up(1 - core))
    own_down = columns(2 * FF, core)
    other_down = columns(2 * FF, 1 - core)
    tokens_other = swapped(tokens)
    hidden = jnp.dot(tokens, own_w, preferred_element_type=jnp.float32)
    hidden, tokens_other = lax.optimization_barrier((hidden, tokens_other))
    hidden = hidden + jnp.dot(tokens_other, other_w, preferred_element_type=jnp.float32)
    act = (jax.nn.silu(hidden[:, :half]) * hidden[:, half:]).astype(jnp.bfloat16)
    out = project_down(act, swapped(act), own_down, other_down)
    home = lax.all_to_all(out, ALL, 0, 0, tiled=True)
    return combined(combine, home, resid)


def solution(mesh):
    finer = Mesh(mesh.devices.reshape(2, 8, 2, 8), ALL)
    return jax.shard_map(
        shards,
        mesh=finer,
        in_specs=(
            P(CTX, "exp"),
            P(CTX, None),
            P(CTX, None),
            P(),
            P(ALL, None),
            P("exp", None, CTX),
            P(),
            P(ALL, None),
            P(ALL, None),
            P("exp", CTX, None),
            P("exp", CTX, None),
            P("exp", CTX, None),
        ),
        out_specs=P(ALL, None),
        check_vma=False,
    )
```

```python
import math

import jax
import jax.numpy as jnp
from jax import lax
from jax.experimental import pallas as pl
from jax.experimental.pallas import tpu as pltpu
from jax.sharding import Mesh
from jax.sharding import PartitionSpec as P


D = 2048
HALF = D // 2
HD = 128
TOPK = 8
SPAN = 64
EXPERTS = 128
OWN = 16
FF = 768
CAP = 2
CHIP = ("yh", "z")
CTX = ("yh", "z", "core")
ALL = ("yh", "z", "core", "exp")
NEG_BIG = -1e30
SWAP = [(0, 1), (1, 0)]


def swapped(x):
    return lax.ppermute(x, "core", SWAP)


def attend_pieces(span_ref, ctx, q_ref, keys, values, o_ref, s_ref):
    rows = q_ref.shape[0]
    part = keys[0].shape[0]
    blocks = part // 128
    q = q_ref[...]
    row = lax.broadcasted_iota(jnp.int32, (rows, 1), 0)
    q_place = jnp.where(
        row < SPAN,
        span_ref[2 * ctx] * SPAN + row,
        span_ref[2 * ctx + 1] * SPAN + row - SPAN,
    )
    lane = lax.broadcasted_iota(jnp.int32, (1, 2 * SPAN), 1)
    dims = (((1,), (1,)), ((), ()))
    top = jnp.full((rows, 128), NEG_BIG, jnp.float32)
    for side in range(4):
        for b in range(blocks):
            k = keys[side][b * 128 : (b + 1) * 128, :]
            s = lax.dot_general(q, k, dims, preferred_element_type=jnp.float32)
            plane, half, z = block_of(ctx, side, b)
            at = 2 * (half * 16 + z * 2 + plane)
            place = jnp.where(
                lane < SPAN,
                span_ref[at] * SPAN + lane,
                span_ref[at + 1] * SPAN + lane - SPAN,
            )
            s = jnp.where(place <= q_place, s, NEG_BIG)
            c0 = (side * blocks + b) * 128
            s_ref[:, c0 : c0 + 128] = s
            top = jnp.maximum(top, s)
    top = jnp.max(top, axis=1, keepdims=True)
    scale = math.log2(math.e) / math.sqrt(HD)
    total = jnp.zeros((rows, 128), jnp.float32)
    acc = jnp.zeros((rows, HD), jnp.float32)
    wide = 512
    for side in range(4):
        for b in range(part // wide):
            c0 = side * part + b * wide
            p = jnp.exp2((s_ref[:, c0 : c0 + wide] - top) * scale)
            for j in range(wide // 128):
                total = total + p[:, j * 128 : (j + 1) * 128]
            v = values[side][b * wide : (b + 1) * wide, :]
            acc = acc + jnp.dot(p.astype(jnp.bfloat16), v, preferred_element_type=jnp.float32)
    o_ref[...] = (acc / jnp.sum(total, axis=1, keepdims=True)).astype(o_ref.dtype)


def attend_kernel(span_ref, where_ref, q_ref, *refs):
    own, cross = refs[0:4], refs[4:8]
    o_ref, s_ref = refs[8:]
    ctx = where_ref[0]

    @pl.when(where_ref[1] == 0)
    def _():
        attend_pieces(span_ref, ctx, q_ref, own, cross, o_ref, s_ref)

    @pl.when(where_ref[1] != 0)
    def _():
        attend_pieces(span_ref, ctx, q_ref, cross, own, o_ref, s_ref)


def attend(span_order, where, queries, own, cross):
    rows, width = queries.shape
    keys = 4 * own[0].shape[0]
    return pl.pallas_call(
        attend_kernel,
        out_shape=jax.ShapeDtypeStruct((rows, width), jnp.bfloat16),
        grid_spec=pltpu.PrefetchScalarGridSpec(
            num_scalar_prefetch=2,
            grid=(width // HD,),
            in_specs=[pl.BlockSpec((rows, HD), lambda h, *_: (0, h))]
            + [pl.BlockSpec(own[0].shape, lambda h, *_: (0, 0))] * 8,
            out_specs=pl.BlockSpec((rows, HD), lambda h, *_: (0, h)),
            scratch_shapes=[pltpu.VMEM((rows, keys), jnp.float32)],
        ),
        cost_estimate=pl.CostEstimate(
            flops=4 * rows * width * keys,
            bytes_accessed=4 * keys * HD + 4 * rows * width,
            transcendentals=rows * keys * width // HD,
        ),
    )(span_order, where, queries, *own, *cross)


def assemble_kernel(*refs):
    parts, (piece_ref, wo_ref) = refs[:5], refs[5:]
    rows = 3 * HD
    at = 0
    for part in parts:
        for first in range(0, part.shape[0], rows):
            piece_ref[at * HD : (at + 1) * HD, :] = part[first : first + HD, :]
            for h in range(4):
                f = first + HD + h * 64
                wo_ref[at * 64 : (at + 1) * 64, h * HD : (h + 1) * HD] = part[f : f + 64, :]
            at += 1


def assembled(parts):
    return pl.pallas_call(
        assemble_kernel,
        out_shape=(
            jax.ShapeDtypeStruct((8 * HD, HD), jnp.bfloat16),
            jax.ShapeDtypeStruct((8 * 64, 4 * HD), jnp.bfloat16),
        ),
        in_specs=[pl.BlockSpec(memory_space=pltpu.VMEM)] * 5,
        out_specs=(pl.BlockSpec(memory_space=pltpu.VMEM),) * 2,
        cost_estimate=pl.CostEstimate(flops=0, bytes_accessed=1572864, transcendentals=0),
    )(*parts)


def block_of(ctx, side, b):
    yh, z, core = ctx // 16, lax.rem(ctx, 16) // 2, lax.rem(ctx, 2)
    half = yh if side % 2 == 0 else 1 - yh
    holder = core if side < 2 else 1 - core
    plane = holder if b in (0, 7) else (b - 1) % 2
    away = (0, 1, 1, 2, 2, 3, 3, 4)[b]
    return plane, half, lax.rem(z + 8 + away * (1 - 2 * holder), 8)


def project_kernel(ctx_ref, x_ref, *refs):
    weights, outs, (w_ref, out_ref) = refs[:4], refs[4:12], refs[12:]
    for side, w in enumerate(weights):
        for b in range(8):
            plane, half, z = block_of(ctx_ref[0], side, b)
            at = pl.multiple_of(plane * HALF + half * (HALF // 2) + z * 64, 64)
            w_ref[pl.ds(at, 64), :] = w[b * 64 : (b + 1) * 64, :]
    out_ref[...] = lax.dot_general(
        x_ref[...], w_ref[...], (((1,), (1,)), ((), ())), preferred_element_type=jnp.float32
    )
    for d, o_ref in enumerate(outs):
        at = pl.multiple_of(jnp.bitwise_xor(ctx_ref[1], d) * 16, 16)
        o_ref[...] = out_ref[pl.ds(at, 16), :].astype(o_ref.dtype)


def project(where, x, weights):
    return pl.pallas_call(
        project_kernel,
        out_shape=(jax.ShapeDtypeStruct((16, D), jnp.bfloat16),) * 8,
        grid_spec=pltpu.PrefetchScalarGridSpec(
            num_scalar_prefetch=1,
            grid=(1,),
            in_specs=[pl.BlockSpec(a.shape, lambda i, *_: (0, 0)) for a in [x, *weights]],
            out_specs=(pl.BlockSpec((16, D), lambda i, *_: (0, 0)),) * 8,
            scratch_shapes=[
                pltpu.VMEM((D, x.shape[1]), jnp.bfloat16),
                pltpu.VMEM((x.shape[0], D), jnp.float32),
            ],
        ),
        cost_estimate=pl.CostEstimate(
            flops=2 * x.shape[0] * x.shape[1] * D, bytes_accessed=2752512, transcendentals=0
        ),
    )(where, x, *weights)


def place_kernel(exp_ref, *refs):
    blocks, (o_ref, row_ref) = refs[:8], refs[8:]
    for d, block in enumerate(blocks):
        row_ref[d * 16 : (d + 1) * 16, :] = block[...].astype(jnp.float32)
    exp = exp_ref[0]
    codes = jnp.transpose(row_ref[:, D:])
    slot = lax.broadcasted_iota(jnp.int32, (256, 128), 0)
    lane = lax.broadcasted_iota(jnp.int32, (256, 128), 1)
    wanted = ((exp * OWN + slot // 16) * CAP + slot % CAP).astype(jnp.float32)
    hit = jnp.zeros((256, 128), jnp.float32)
    for t in range(TOPK):
        hit = hit + jnp.where(codes[t : t + 1, :] == wanted, 1.0, 0.0)
    hit = jnp.where((slot % 16) // CAP == jnp.bitwise_xor(lane // 16, exp), hit, 0.0)
    hit = hit.astype(jnp.bfloat16)
    for plane in range(2):
        x = row_ref[:, plane * HALF : (plane + 1) * HALF].astype(jnp.bfloat16)
        out = jnp.dot(hit, x, preferred_element_type=jnp.float32).astype(o_ref.dtype)
        for k in range(OWN):
            o_ref[2 * k + plane, :, :] = out[k * 16 : (k + 1) * 16, :]


def placed(exp, blocks):
    return pl.pallas_call(
        place_kernel,
        out_shape=jax.ShapeDtypeStruct((2 * OWN, 16, HALF), jnp.bfloat16),
        grid_spec=pltpu.PrefetchScalarGridSpec(
            num_scalar_prefetch=1,
            grid=(1,),
            in_specs=[pl.BlockSpec(b.shape, lambda i, *_: (0, 0)) for b in blocks],
            out_specs=pl.BlockSpec((2 * OWN, 16, HALF), lambda i, *_: (0, 0, 0)),
            scratch_shapes=[pltpu.VMEM((128, D + 128), jnp.float32)],
        ),
        cost_estimate=pl.CostEstimate(
            flops=2 * 256 * 128 * D, bytes_accessed=1605632, transcendentals=0
        ),
    )(exp[None].astype(jnp.int32), *blocks)


def across_y(x):
    return lax.ppermute(x, "yh", SWAP)


def across_x(x):
    return lax.ppermute(x, "exp", [(e, e ^ 1) for e in range(8)])


def across_xy(x):
    pairs = [(y * 8 + e, (1 - y) * 8 + (e ^ 1)) for y in range(2) for e in range(8)]
    return lax.ppermute(x, ("yh", "exp"), pairs)


def by_plane(x):
    rows = x.shape[0]
    return x.reshape(rows, D // 128, 2, 64).transpose(0, 2, 1, 3).reshape(rows, D)


def from_planes(x):
    rows = x.shape[0]
    return x.reshape(rows, 2, D // 128, 64).transpose(0, 2, 1, 3).reshape(rows, D)


def shards(
    queries,
    keys,
    values,
    span_order,
    stream_in,
    wo,
    norm_gain,
    expert_ids,
    expert_gates,
    w_gate,
    w_up,
    w_down,
):
    core = lax.axis_index("core")
    ctx = lax.axis_index(CTX)
    exp = lax.axis_index("exp")

    head = exp // 2 * HD
    mine = jnp.where(
        exp % 2 == 0,
        lax.dynamic_slice_in_dim(keys, head, HD, 1),
        lax.dynamic_slice_in_dim(values, head, HD, 1),
    )
    packed = jnp.concatenate([mine, wo.transpose(0, 2, 1).reshape(-1, HD)], axis=0)
    other = swapped(packed)
    both = jnp.concatenate(
        [jnp.where(core == 0, packed, other), jnp.where(core == 0, other, packed)], axis=0
    )
    parts = [packed]
    for j in range(1, 4):
        pairs = [
            ((i + (j if c == 0 else 8 - j)) % 8 * 2 + c, i * 2 + c)
            for i in range(8)
            for c in range(2)
        ]
        parts.append(lax.ppermute(both, ("z", "core"), pairs))
    parts.append(lax.ppermute(packed, "z", [((i + 4) % 8, i) for i in range(8)]))
    weights = lax.all_to_all(
        jnp.concatenate([w_gate, w_up, w_down], axis=2), CHIP, 0, 0, tiled=True
    ).reshape(HALF, -1)

    piece, wo_near = assembled(parts)
    near = [piece, across_y(piece), across_x(piece), across_xy(piece)]
    wo_near = [wo_near, across_y(wo_near)]
    far = [swapped(p) for p in near]
    wo_far = [swapped(w) for w in wo_near]

    attended = attend(
        span_order,
        jnp.stack([ctx, exp % 2]).astype(jnp.int32),
        queries,
        near[0:2] + far[0:2],
        near[2:4] + far[2:4],
    )
    where = jnp.stack([ctx, exp]).astype(jnp.int32)
    mixed = project(where, attended, wo_near + wo_far)
    summed = mixed[0].astype(jnp.float32)
    for d in range(1, 8):
        got = lax.ppermute(mixed[d], "exp", [(e, e ^ d) for e in range(8)])
        summed = summed + got.astype(jnp.float32)
    resid = by_plane(stream_in.astype(jnp.float32)) + summed
    gain = by_plane(norm_gain.astype(jnp.float32)[None])
    normed = (
        resid
        * lax.rsqrt(jnp.mean(resid * resid, axis=-1, keepdims=True) + 1e-06)
        * gain
    ).astype(jnp.bfloat16)

    rows = stream_in.shape[0]
    flat = expert_ids.reshape(-1)
    hits = (flat[:, None] == jnp.arange(EXPERTS, dtype=jnp.int32)[None, :]).astype(jnp.float32)
    before = (
        jnp.arange(rows * TOPK)[:, None] > jnp.arange(rows * TOPK)[None, :]
    ).astype(jnp.float32)
    ahead = jnp.dot(before, hits, preferred_element_type=jnp.float32)
    rank = jnp.sum(ahead * hits, axis=1).astype(jnp.int32)
    slots = (((flat % OWN) * 8 + flat // OWN) * CAP + rank).reshape(rows, TOPK)
    slot_ids = jnp.arange(EXPERTS * CAP, dtype=jnp.int32)
    codes = (flat * CAP + rank).reshape(rows, TOPK).astype(jnp.bfloat16)
    codes = jnp.pad(codes, ((0, 0), (0, 128 - TOPK)))
    combine = jnp.sum(
        jnp.where(
            slots[:, :, None] == slot_ids[None, None, :],
            expert_gates[:, :, None],
            jnp.zeros((), jnp.bfloat16),
        ),
        axis=1,
    )

    payload = jnp.concatenate([normed, codes], axis=1)
    blocks = [payload] + [
        lax.ppermute(payload, "exp", [(e, e ^ d) for e in range(8)]) for d in range(1, 8)
    ]
    outgoing = placed(exp, blocks)
    tokens = lax.all_to_all(outgoing, CTX, 0, 0, tiled=True).reshape(512, HALF)

    half = FF // 2

    def columns(first, at):
        return lax.dynamic_slice_in_dim(weights, first + at * half, half, 1)

    def gate_up(at):
        return jnp.concatenate([columns(0, at), columns(FF, at)], axis=1)

    own_w = gate_up(core)
    other_w = swapped(gate_up(1 - core))
    own_down = columns(2 * FF, core)
    other_down = columns(2 * FF, 1 - core)
    tokens_other = swapped(tokens)
    hidden = jnp.dot(tokens, own_w, preferred_element_type=jnp.float32)
    hidden, tokens_other = lax.optimization_barrier((hidden, tokens_other))
    hidden = hidden + jnp.dot(tokens_other, other_w, preferred_element_type=jnp.float32)
    act = (jax.nn.silu(hidden[:, :half]) * hidden[:, half:]).astype(jnp.bfloat16)
    dims = (((1,), (1,)), ((), ()))
    act_other = swapped(act)
    out = lax.dot_general(act, own_down, dims, preferred_element_type=jnp.float32)
    out, act_other = lax.optimization_barrier((out, act_other))
    out = out + lax.dot_general(act_other, other_down, dims, preferred_element_type=jnp.float32)
    out = out.astype(jnp.bfloat16)
    home = lax.all_to_all(out.reshape(256, CAP, HALF), ALL, 0, 0, tiled=True)
    home = home.reshape(OWN, 2, 8, CAP, HALF).transpose(0, 2, 3, 1, 4).reshape(EXPERTS * CAP, D)
    moe = jnp.dot(combine, home, preferred_element_type=jnp.float32)
    return from_planes(resid + moe)


def solution(mesh):
    finer = Mesh(mesh.devices.reshape(2, 8, 2, 8), ALL)
    return jax.shard_map(
        shards,
        mesh=finer,
        in_specs=(
            P(CTX, "exp"),
            P(CTX, None),
            P(CTX, None),
            P(),
            P(ALL, None),
            P("exp", None, CTX),
            P(),
            P(ALL, None),
            P(ALL, None),
            P("exp", CTX, None),
            P("exp", CTX, None),
            P("exp", CTX, None),
        ),
        out_specs=P(ALL, None),
        check_vma=False,
    )
```

```python
import math

import jax
import jax.numpy as jnp
from jax import lax
from jax.experimental import pallas as pl
from jax.experimental.pallas import tpu as pltpu
from jax.sharding import Mesh
from jax.sharding import PartitionSpec as P


D = 2048
HALF = D // 2
HD = 128
TOPK = 8
SPAN = 64
EXPERTS = 128
OWN = 16
FF = 768
CAP = 2
CHIP = ("yh", "z")
CTX = ("yh", "z", "core")
ALL = ("yh", "z", "core", "exp")
NEG_BIG = -1e30
SWAP = [(0, 1), (1, 0)]


def swapped(x):
    return lax.ppermute(x, "core", SWAP)


def attend_pieces(span_ref, ctx, q_ref, keys, values, o_ref, s_ref):
    rows = q_ref.shape[0]
    part = keys[0].shape[0]
    blocks = part // 128
    q = q_ref[...]
    row = lax.broadcasted_iota(jnp.int32, (rows, 1), 0)
    q_place = jnp.where(
        row < SPAN,
        span_ref[2 * ctx] * SPAN + row,
        span_ref[2 * ctx + 1] * SPAN + row - SPAN,
    )
    lane = lax.broadcasted_iota(jnp.int32, (1, 2 * SPAN), 1)
    dims = (((1,), (1,)), ((), ()))
    top = jnp.full((rows, 128), NEG_BIG, jnp.float32)
    for side in range(4):
        for b in range(blocks):
            k = keys[side][b * 128 : (b + 1) * 128, :]
            s = lax.dot_general(q, k, dims, preferred_element_type=jnp.float32)
            plane, half, z = block_of(ctx, side, b)
            at = 2 * (half * 16 + z * 2 + plane)
            place = jnp.where(
                lane < SPAN,
                span_ref[at] * SPAN + lane,
                span_ref[at + 1] * SPAN + lane - SPAN,
            )
            s = jnp.where(place <= q_place, s, NEG_BIG)
            c0 = (side * blocks + b) * 128
            s_ref[:, c0 : c0 + 128] = s
            top = jnp.maximum(top, s)
    top = jnp.max(top, axis=1, keepdims=True)
    scale = math.log2(math.e) / math.sqrt(HD)
    total = jnp.zeros((rows, 128), jnp.float32)
    acc = jnp.zeros((rows, HD), jnp.float32)
    wide = 512
    for side in range(4):
        for b in range(part // wide):
            c0 = side * part + b * wide
            p = jnp.exp2((s_ref[:, c0 : c0 + wide] - top) * scale)
            for j in range(wide // 128):
                total = total + p[:, j * 128 : (j + 1) * 128]
            v = values[side][b * wide : (b + 1) * wide, :]
            acc = acc + jnp.dot(p.astype(jnp.bfloat16), v, preferred_element_type=jnp.float32)
    o_ref[...] = (acc / jnp.sum(total, axis=1, keepdims=True)).astype(o_ref.dtype)


def attend_kernel(span_ref, where_ref, q_ref, *refs):
    own, cross = refs[0:4], refs[4:8]
    o_ref, s_ref = refs[8:]
    ctx = where_ref[0]

    @pl.when(where_ref[1] == 0)
    def _():
        attend_pieces(span_ref, ctx, q_ref, own, cross, o_ref, s_ref)

    @pl.when(where_ref[1] != 0)
    def _():
        attend_pieces(span_ref, ctx, q_ref, cross, own, o_ref, s_ref)


def attend(span_order, where, queries, own, cross):
    rows, width = queries.shape
    keys = 4 * own[0].shape[0]
    return pl.pallas_call(
        attend_kernel,
        out_shape=jax.ShapeDtypeStruct((rows, width), jnp.bfloat16),
        grid_spec=pltpu.PrefetchScalarGridSpec(
            num_scalar_prefetch=2,
            grid=(width // HD,),
            in_specs=[pl.BlockSpec((rows, HD), lambda h, *_: (0, h))]
            + [pl.BlockSpec(own[0].shape, lambda h, *_: (0, 0))] * 8,
            out_specs=pl.BlockSpec((rows, HD), lambda h, *_: (0, h)),
            scratch_shapes=[pltpu.VMEM((rows, keys), jnp.float32)],
        ),
        cost_estimate=pl.CostEstimate(
            flops=4 * rows * width * keys,
            bytes_accessed=4 * keys * HD + 4 * rows * width,
            transcendentals=rows * keys * width // HD,
        ),
    )(span_order, where, queries, *own, *cross)


def assemble_kernel(*refs):
    parts, (piece_ref, wo_ref) = refs[:5], refs[5:]
    rows = 3 * HD
    at = 0
    for part in parts:
        for first in range(0, part.shape[0], rows):
            piece_ref[at * HD : (at + 1) * HD, :] = part[first : first + HD, :]
            for h in range(4):
                f = first + HD + h * 64
                wo_ref[at * 64 : (at + 1) * 64, h * HD : (h + 1) * HD] = part[f : f + 64, :]
            at += 1


def assembled(parts):
    return pl.pallas_call(
        assemble_kernel,
        out_shape=(
            jax.ShapeDtypeStruct((8 * HD, HD), jnp.bfloat16),
            jax.ShapeDtypeStruct((8 * 64, 4 * HD), jnp.bfloat16),
        ),
        in_specs=[pl.BlockSpec(memory_space=pltpu.VMEM)] * 5,
        out_specs=(pl.BlockSpec(memory_space=pltpu.VMEM),) * 2,
        cost_estimate=pl.CostEstimate(flops=0, bytes_accessed=1572864, transcendentals=0),
    )(*parts)


def block_of(ctx, side, b):
    yh, z, core = ctx // 16, lax.rem(ctx, 16) // 2, lax.rem(ctx, 2)
    half = yh if side % 2 == 0 else 1 - yh
    holder = core if side < 2 else 1 - core
    plane = holder if b in (0, 7) else (b - 1) % 2
    away = (0, 1, 1, 2, 2, 3, 3, 4)[b]
    return plane, half, lax.rem(z + 8 + away * (1 - 2 * holder), 8)


def project_kernel(ctx_ref, x_ref, *refs):
    weights, outs, (w_ref, out_ref) = refs[:4], refs[4:12], refs[12:]
    for side, w in enumerate(weights):
        for b in range(8):
            plane, half, z = block_of(ctx_ref[0], side, b)
            at = pl.multiple_of(plane * HALF + half * (HALF // 2) + z * 64, 64)
            w_ref[pl.ds(at, 64), :] = w[b * 64 : (b + 1) * 64, :]
    out_ref[...] = lax.dot_general(
        x_ref[...], w_ref[...], (((1,), (1,)), ((), ())), preferred_element_type=jnp.float32
    )
    for d, o_ref in enumerate(outs):
        at = pl.multiple_of(jnp.bitwise_xor(ctx_ref[1], d) * 16, 16)
        o_ref[...] = out_ref[pl.ds(at, 16), :].astype(o_ref.dtype)


def project(where, x, weights):
    return pl.pallas_call(
        project_kernel,
        out_shape=(jax.ShapeDtypeStruct((16, D), jnp.bfloat16),) * 8,
        grid_spec=pltpu.PrefetchScalarGridSpec(
            num_scalar_prefetch=1,
            grid=(1,),
            in_specs=[pl.BlockSpec(a.shape, lambda i, *_: (0, 0)) for a in [x, *weights]],
            out_specs=(pl.BlockSpec((16, D), lambda i, *_: (0, 0)),) * 8,
            scratch_shapes=[
                pltpu.VMEM((D, x.shape[1]), jnp.bfloat16),
                pltpu.VMEM((x.shape[0], D), jnp.float32),
            ],
        ),
        cost_estimate=pl.CostEstimate(
            flops=2 * x.shape[0] * x.shape[1] * D, bytes_accessed=2752512, transcendentals=0
        ),
    )(where, x, *weights)


def place_kernel(exp_ref, *refs):
    blocks, (o_ref, row_ref) = refs[:8], refs[8:]
    for d, block in enumerate(blocks):
        row_ref[d * 16 : (d + 1) * 16, :] = block[...]
    exp = exp_ref[0]
    codes = jnp.transpose(row_ref[:, D:].astype(jnp.float32))
    slot = lax.broadcasted_iota(jnp.int32, (256, 128), 0)
    lane = lax.broadcasted_iota(jnp.int32, (256, 128), 1)
    wanted = ((exp * OWN + slot // 16) * CAP + slot % CAP).astype(jnp.float32)
    hit = jnp.zeros((256, 128), jnp.float32)
    for t in range(TOPK):
        hit = hit + jnp.where(codes[t : t + 1, :] == wanted, 1.0, 0.0)
    hit = jnp.where((slot % 16) // CAP == jnp.bitwise_xor(lane // 16, exp), hit, 0.0)
    hit = hit.astype(jnp.bfloat16)
    for plane in range(2):
        x = row_ref[:, plane * HALF : (plane + 1) * HALF]
        out = jnp.dot(hit, x, preferred_element_type=jnp.float32).astype(o_ref.dtype)
        for k in range(OWN):
            o_ref[2 * k + plane, :, :] = out[k * 16 : (k + 1) * 16, :]


def placed(exp, blocks):
    return pl.pallas_call(
        place_kernel,
        out_shape=jax.ShapeDtypeStruct((2 * OWN, 16, HALF), jnp.bfloat16),
        grid_spec=pltpu.PrefetchScalarGridSpec(
            num_scalar_prefetch=1,
            grid=(1,),
            in_specs=[pl.BlockSpec(b.shape, lambda i, *_: (0, 0)) for b in blocks],
            out_specs=pl.BlockSpec((2 * OWN, 16, HALF), lambda i, *_: (0, 0, 0)),
            scratch_shapes=[pltpu.VMEM((128, D + 128), jnp.bfloat16)],
        ),
        cost_estimate=pl.CostEstimate(
            flops=2 * 256 * 128 * D, bytes_accessed=1605632, transcendentals=0
        ),
    )(exp[None].astype(jnp.int32), *blocks)


def across_y(x):
    return lax.ppermute(x, "yh", SWAP)


def across_x(x):
    return lax.ppermute(x, "exp", [(e, e ^ 1) for e in range(8)])


def across_xy(x):
    pairs = [(y * 8 + e, (1 - y) * 8 + (e ^ 1)) for y in range(2) for e in range(8)]
    return lax.ppermute(x, ("yh", "exp"), pairs)


def by_plane(x):
    rows = x.shape[0]
    return x.reshape(rows, D // 128, 2, 64).transpose(0, 2, 1, 3).reshape(rows, D)


def from_planes(x):
    rows = x.shape[0]
    return x.reshape(rows, 2, D // 128, 64).transpose(0, 2, 1, 3).reshape(rows, D)


def shards(
    queries,
    keys,
    values,
    span_order,
    stream_in,
    wo,
    norm_gain,
    expert_ids,
    expert_gates,
    w_gate,
    w_up,
    w_down,
):
    core = lax.axis_index("core")
    ctx = lax.axis_index(CTX)
    exp = lax.axis_index("exp")

    head = exp // 2 * HD
    mine = jnp.where(
        exp % 2 == 0,
        lax.dynamic_slice_in_dim(keys, head, HD, 1),
        lax.dynamic_slice_in_dim(values, head, HD, 1),
    )
    packed = jnp.concatenate([mine, wo.transpose(0, 2, 1).reshape(-1, HD)], axis=0)
    other = swapped(packed)
    both = jnp.concatenate(
        [jnp.where(core == 0, packed, other), jnp.where(core == 0, other, packed)], axis=0
    )
    parts = [packed]
    for j in range(1, 4):
        pairs = [
            ((i + (j if c == 0 else 8 - j)) % 8 * 2 + c, i * 2 + c)
            for i in range(8)
            for c in range(2)
        ]
        parts.append(lax.ppermute(both, ("z", "core"), pairs))
    parts.append(lax.ppermute(packed, "z", [((i + 4) % 8, i) for i in range(8)]))
    weights = lax.all_to_all(
        jnp.concatenate([w_gate, w_up, w_down], axis=2), CHIP, 0, 0, tiled=True
    ).reshape(HALF, -1)

    piece, wo_near = assembled(parts)
    near = [piece, across_y(piece), across_x(piece), across_xy(piece)]
    wo_near = [wo_near, across_y(wo_near)]
    far = [swapped(p) for p in near]
    wo_far = [swapped(wo_near[0])]
    wo_far.append(swapped(wo_near[1]))

    attended = attend(
        span_order,
        jnp.stack([ctx, exp % 2]).astype(jnp.int32),
        queries,
        near[0:2] + far[0:2],
        near[2:4] + far[2:4],
    )
    where = jnp.stack([ctx, exp]).astype(jnp.int32)
    mixed = project(where, attended, wo_near + wo_far)
    summed = mixed[0].astype(jnp.float32)
    for d in range(1, 8):
        got = lax.ppermute(mixed[d], "exp", [(e, e ^ d) for e in range(8)])
        summed = summed + got.astype(jnp.float32)
    resid = by_plane(stream_in.astype(jnp.float32)) + summed
    gain = by_plane(norm_gain.astype(jnp.float32)[None])
    normed = (
        resid
        * lax.rsqrt(jnp.mean(resid * resid, axis=-1, keepdims=True) + 1e-06)
        * gain
    ).astype(jnp.bfloat16)

    rows = stream_in.shape[0]
    flat = expert_ids.reshape(-1)
    hits = (flat[:, None] == jnp.arange(EXPERTS, dtype=jnp.int32)[None, :]).astype(jnp.float32)
    before = (
        jnp.arange(rows * TOPK)[:, None] > jnp.arange(rows * TOPK)[None, :]
    ).astype(jnp.float32)
    ahead = jnp.dot(before, hits, preferred_element_type=jnp.float32)
    rank = jnp.sum(ahead * hits, axis=1).astype(jnp.int32)
    slots = (((flat % OWN) * 8 + flat // OWN) * CAP + rank).reshape(rows, TOPK)
    slot_ids = jnp.arange(EXPERTS * CAP, dtype=jnp.int32)
    codes = (flat * CAP + rank).reshape(rows, TOPK).astype(jnp.bfloat16)
    codes = jnp.pad(codes, ((0, 0), (0, 128 - TOPK)))
    combine = jnp.sum(
        jnp.where(
            slots[:, :, None] == slot_ids[None, None, :],
            expert_gates[:, :, None],
            jnp.zeros((), jnp.bfloat16),
        ),
        axis=1,
    )

    payload = jnp.concatenate([normed, codes], axis=1)
    blocks = [payload] + [
        lax.ppermute(payload, "exp", [(e, e ^ d) for e in range(8)]) for d in range(1, 8)
    ]
    outgoing = placed(exp, blocks)
    tokens = lax.all_to_all(outgoing, CTX, 0, 0, tiled=True).reshape(512, HALF)

    half = FF // 2

    def columns(first, at):
        return lax.dynamic_slice_in_dim(weights, first + at * half, half, 1)

    def gate_up(at):
        return jnp.concatenate([columns(0, at), columns(FF, at)], axis=1)

    own_w = gate_up(core)
    other_w = swapped(gate_up(1 - core))
    own_down = columns(2 * FF, core)
    other_down = columns(2 * FF, 1 - core)
    tokens_other = swapped(tokens)
    hidden = jnp.dot(tokens, own_w, preferred_element_type=jnp.float32)
    hidden, tokens_other = lax.optimization_barrier((hidden, tokens_other))
    hidden = hidden + jnp.dot(tokens_other, other_w, preferred_element_type=jnp.float32)
    act = (jax.nn.silu(hidden[:, :half]) * hidden[:, half:]).astype(jnp.bfloat16)
    dims = (((1,), (1,)), ((), ()))
    act_other = swapped(act)
    out = lax.dot_general(act, own_down, dims, preferred_element_type=jnp.float32)
    out, act_other = lax.optimization_barrier((out, act_other))
    out = out + lax.dot_general(act_other, other_down, dims, preferred_element_type=jnp.float32)
    out = out.astype(jnp.bfloat16)
    home = lax.all_to_all(out.reshape(256, CAP, HALF), ALL, 0, 0, tiled=True)
    home = home.reshape(OWN, 2, 8, CAP, HALF).transpose(0, 2, 3, 1, 4).reshape(EXPERTS * CAP, D)
    moe = jnp.dot(combine, home, preferred_element_type=jnp.float32)
    return from_planes(resid + moe)


def solution(mesh):
    finer = Mesh(mesh.devices.reshape(2, 8, 2, 8), ALL)
    return jax.shard_map(
        shards,
        mesh=finer,
        in_specs=(
            P(CTX, "exp"),
            P(CTX, None),
            P(CTX, None),
            P(),
            P(ALL, None),
            P("exp", None, CTX),
            P(),
            P(ALL, None),
            P(ALL, None),
            P("exp", CTX, None),
            P("exp", CTX, None),
            P("exp", CTX, None),
        ),
        out_specs=P(ALL, None),
        check_vma=False,
    )
```
